128 devices in a mesh: grp: 4 (over y_hi, core), row: 4 (over z), col: 8 (over x, y_lo).
Axes of the slice: x: 4, y: 4 (y_hi: 2, y_lo: 2; y = y_hi * 2 + y_lo), z: 4, core: 2. Of those that a mesh axis runs over, the one named last changes fastest.
Arguments:
- pair_rep: bfloat16 [4, 512, 512, 128], P('grp', 'row', 'col'), may hold values from -6 to 6
- cotangent: bfloat16 [4, 512, 512, 128], P('grp', 'row', 'col'), may hold values from -6 to 6
- lengths: int32 [4], replicated, may hold values from 128 to 512, as said below
- weight_in: bfloat16 [128, 640], replicated, may hold values from -0.5 to 0.5
- weight_out: bfloat16 [128, 128], replicated, may hold values from -0.5 to 0.5
- gain_in: float32 [128], replicated, may hold values from 0.1 to 1.9
- gain_out: float32 [128], replicated, may hold values from 0.1 to 1.9
Outputs:
- mixed: bfloat16 [4, 512, 512, 128], P('grp', 'row', 'col')
- grad_pair: bfloat16 [4, 512, 512, 128], P('grp', 'row', 'col')
- grad_weight_in: float32 [128, 640], replicated
- grad_weight_out: float32 [128, 128], replicated
- grad_gain_in: float32 [128], replicated
- grad_gain_out: float32 [128], replicated
The draws below stay inside these ranges and needn't reach their ends.
Inputs may be any that keep to these rules, and one draw needn't show every extreme that they name: `lengths`: in every draw one complex has exactly 512 real residues and another exactly 128.
All inputs are finite; a program needn't handle non-finite values.
Results may differ from the reference program's by a relative error of at most 0.0089.
Values may be sent and summed in bfloat16 or wider, within the bound.
No kernel may reach another device: no remote copies, remote signals or barrier semaphores. Data moves between devices by JAX's collectives and lax.ppermute only.
A program may use at most 128 MiB of HBM per device.

```python
import jax
import jax.numpy as jnp
from jax import lax

C = 128
H = 128
N = 512
GROUPS = 4


def draw_lengths(key, part):
    base = jax.random.fold_in(key, 11)
    key_values, key_full, key_short = jax.random.split(base, 3)
    values = jax.random.randint(key_values, (GROUPS,), N // 4, N + 1)
    fullest = jax.random.randint(key_full, (), 0, GROUPS)
    shortest = (fullest + jax.random.randint(key_short, (), 1, GROUPS)) % GROUPS
    slots = jnp.arange(GROUPS)
    values = jnp.where(slots == fullest, N, values)
    values = jnp.where(slots == shortest, N // 4, values)
    return values.astype(jnp.int32)


def shard_levels(key, dims, cuts, least, largest):
    factor_of = 1.0
    for axis_at, shards_of in cuts:
        steps = jax.random.uniform(jax.random.fold_in(jax.random.fold_in(key, 6), axis_at), (shards_of,), jnp.float32, least / len(cuts), largest / len(cuts))
        factor_of = factor_of * jnp.repeat(jnp.exp(steps), dims[axis_at] // shards_of).reshape((-1,) + (1,) * (len(dims) - 1 - axis_at))
    return factor_of


def scatter_about(own_key, extent, deviation, bound, cuts=(), held_as=jnp.bfloat16):
    values = jax.random.normal(own_key, extent, jnp.float32) * deviation
    if len(cuts) > 0:
        values = shard_levels(own_key, extent, cuts, -0.22, 0.18) * values
    return jnp.clip(values, min=-bound, max=bound).astype(held_as)


def setup_inputs(seed: int = 0) -> dict:
    key_list = jax.random.split(jax.random.key(seed), 8)
    return {
        "pair_rep": scatter_about(key_list[0], (GROUPS, N, N, C), 1.0, 6.0, ((0, 4), (1, 4), (2, 8))),
        "cotangent": scatter_about(key_list[1], (GROUPS, N, N, C), 1.0, 6.0, ((0, 4), (1, 4), (2, 8))),
        "lengths": draw_lengths(jax.random.fold_in(key_list[7], 71), 0),
        "weight_in": scatter_about(key_list[3], (C, 4 * H + C), C ** -0.5, 0.5),
        "weight_out": scatter_about(key_list[4], (H, C), H ** -0.5, 0.5),
        "gain_in": jnp.clip(1.0 + 0.18 * jax.random.normal(key_list[5], (C,), jnp.float32), 0.1, 1.9),
        "gain_out": jnp.clip(1.0 + 0.18 * jax.random.normal(key_list[6], (H,), jnp.float32), 0.1, 1.9),
    }


epsilon = 1e-05

def normalize(values, along):
    centred = values - lax.optimization_barrier(jnp.mean(values, axis=along, keepdims=True))
    inverse = lax.rsqrt(lax.optimization_barrier(jnp.mean(centred * centred, axis=along, keepdims=True)) + epsilon)
    return (centred * inverse, inverse)

def normalize_back(grad_hat, normed, inverse, along):
    first_mean = lax.optimization_barrier(jnp.mean(grad_hat, axis=along, keepdims=True))
    second_mean = lax.optimization_barrier(jnp.mean(grad_hat * normed, axis=along, keepdims=True))
    return inverse * (grad_hat - first_mean - normed * second_mean)

def settle(values):
    return lax.optimization_barrier(values.astype(jnp.bfloat16)).astype(jnp.float32)

def one_complex(pair_rep, cotangent, length, weight_in, weight_out, gain_in, gain_out):
    hidden_width = weight_out.shape[0]
    positions = jnp.arange(N)
    inside = ((positions[:, None] < length) & (positions[None, :] < length)).astype(jnp.float32)[:, :, None]
    z_hat, z_inverse = normalize(pair_rep.astype(jnp.float32), -1)
    z_norm = (z_hat * gain_in).astype(jnp.bfloat16)
    projected = jnp.dot(z_norm, weight_in, preferred_element_type=jnp.float32)
    left_lin = projected[:, :, 0:hidden_width]
    left_pre = projected[:, :, hidden_width:2 * hidden_width]
    right_lin = projected[:, :, 2 * hidden_width:3 * hidden_width]
    right_pre = projected[:, :, 3 * hidden_width:4 * hidden_width]
    gate_pre = projected[:, :, 4 * hidden_width:]
    left_sig = jax.nn.sigmoid(left_pre)
    right_sig = jax.nn.sigmoid(right_pre)
    left_vals = settle(left_sig * left_lin * inside)
    right_vals = settle(right_sig * right_lin * inside)
    outer_prod = settle(jnp.einsum('ikh,jkh->ijh', left_vals, right_vals))
    o_hat, o_inverse = normalize(outer_prod, -1)
    o_norm = (o_hat * gain_out).astype(jnp.bfloat16)
    proj_out = jnp.dot(o_norm, weight_out, preferred_element_type=jnp.float32)
    gate = jax.nn.sigmoid(gate_pre)
    mixed = (gate * proj_out * inside).astype(jnp.bfloat16)
    grad_out = cotangent.astype(jnp.float32)
    grad_proj = (grad_out * gate * inside).astype(jnp.bfloat16)
    grad_gate = (grad_out * proj_out * inside * gate * (1.0 - gate)).astype(jnp.bfloat16)
    grad_w_out = jnp.einsum('ijh,ijc->hc', o_norm.astype(jnp.float32), grad_proj.astype(jnp.float32))
    grad_o_norm = jnp.dot(grad_proj, weight_out.T, preferred_element_type=jnp.float32)
    grad_g_out = lax.optimization_barrier(jnp.sum(grad_o_norm * o_hat, axis=(0, 1)))
    grad_outer = settle(normalize_back(grad_o_norm * gain_out, o_hat, o_inverse, -1))
    grad_left = settle(jnp.einsum('ijh,jkh->ikh', grad_outer, right_vals))
    grad_right = settle(jnp.einsum('ijh,ikh->jkh', grad_outer, left_vals))
    d_left_lin = grad_left * left_sig * inside
    d_left_pre = grad_left * left_lin * inside * left_sig * (1.0 - left_sig)
    d_right_lin = grad_right * right_sig * inside
    d_right_pre = grad_right * right_lin * inside * right_sig * (1.0 - right_sig)
    grad_proj_in = jnp.concatenate([d_left_lin, d_left_pre, d_right_lin, d_right_pre, grad_gate.astype(jnp.float32)], -1).astype(jnp.bfloat16)
    grad_z_norm = jnp.dot(grad_proj_in, weight_in.T, preferred_element_type=jnp.float32)
    grad_w_in = jnp.einsum('ijc,ijq->cq', z_norm.astype(jnp.float32), grad_proj_in.astype(jnp.float32))
    grad_g_in = lax.optimization_barrier(jnp.sum(grad_z_norm * z_hat, axis=(0, 1)))
    grad_pair = normalize_back(grad_z_norm * gain_in, z_hat, z_inverse, -1).astype(jnp.bfloat16)
    return (mixed, grad_pair, grad_w_in, grad_w_out, grad_g_in, grad_g_out)

def reference(pair_rep, cotangent, lengths, weight_in, weight_out, gain_in, gain_out):
    mixed_list = []
    grad_list = []
    sums = None
    for group in range(GROUPS):
        result = one_complex(pair_rep[group], cotangent[group], lengths[group], weight_in, weight_out, gain_in, gain_out)
        mixed_list.append(result[0])
        grad_list.append(result[1])
        if sums is None:
            sums = list(result[2:])
        else:
            sums = [running + extra for running, extra in zip(sums, result[2:])]
    return (jnp.stack(mixed_list), jnp.stack(grad_list), sums[0] / N, sums[1] / N, sums[2] / N, sums[3] / N)
```

```python
import functools

import jax
import jax.numpy as jnp
from jax import lax
from jax.experimental import pallas as pl
from jax.experimental.pallas import tpu as pltpu
from jax.sharding import PartitionSpec as P

N = 512
ALL = ("grp", "row", "col")
TILE = ("row", "col")


epsilon = 1e-05


def normalize(values, along):
    centred = values - jnp.mean(values, axis=along, keepdims=True)
    inverse = lax.rsqrt(jnp.mean(centred * centred, axis=along, keepdims=True) + epsilon)
    return (centred * inverse, inverse)


def normalize_back(grad_hat, normed, inverse, along):
    first_mean = jnp.mean(grad_hat, axis=along, keepdims=True)
    second_mean = jnp.mean(grad_hat * normed, axis=along, keepdims=True)
    return inverse * (grad_hat - first_mean - normed * second_mean)


def exchange(tiles):
    return lax.all_to_all(tiles, TILE, split_axis=0, concat_axis=0, tiled=True)


def forward_kernel(rows_n, cols_n, pair_ref, out_ref, left_ref, right_ref):
    col_len, row_len = pair_ref.shape[3], pair_ref.shape[4]
    for r in range(rows_n):
        for c in range(cols_n):
            at = (pl.ds(c * col_len, col_len), pl.ds(r * row_len, row_len))
            left_ref[at] = pair_ref[r * cols_n + c, 0, 0]
            right_ref[at] = pair_ref[r * cols_n + c, 0, 1]
    outer = lax.dot_general(
        right_ref[...], left_ref[...], (((0,), (0,)), ((), ())), preferred_element_type=jnp.float32
    ).astype(jnp.bfloat16)
    for r in range(rows_n):
        for c in range(cols_n):
            out_ref[r * cols_n + c, 0] = outer[
                c * col_len : (c + 1) * col_len, r * row_len : (r + 1) * row_len
            ]


def backward_kernel(rows_n, cols_n, pair_ref, grad_ref, out_ref, left_ref, right_ref, outer_ref):
    col_len, row_len = pair_ref.shape[3], pair_ref.shape[4]
    for r in range(rows_n):
        for c in range(cols_n):
            at = (pl.ds(c * col_len, col_len), pl.ds(r * row_len, row_len))
            left_ref[at] = pair_ref[r * cols_n + c, 0, 0]
            right_ref[at] = pair_ref[r * cols_n + c, 0, 1]
            outer_ref[at] = grad_ref[r * cols_n + c, 0]
    grad_left = lax.dot_general(
        right_ref[...], outer_ref[...], (((1,), (0,)), ((), ())), preferred_element_type=jnp.float32
    ).astype(jnp.bfloat16)
    grad_right = lax.dot_general(
        left_ref[...], outer_ref[...], (((1,), (1,)), ((), ())), preferred_element_type=jnp.float32
    ).astype(jnp.bfloat16)
    for r in range(rows_n):
        for c in range(cols_n):
            at = (slice(c * col_len, (c + 1) * col_len), slice(r * row_len, (r + 1) * row_len))
            out_ref[r * cols_n + c, 0, 0] = grad_left[at]
            out_ref[r * cols_n + c, 0, 1] = grad_right[at]


def triangle(pair_ch, rows_n, cols_n):
    devices, share, _, col_len, row_len = pair_ch.shape
    side = cols_n * col_len
    return pl.pallas_call(
        functools.partial(forward_kernel, rows_n, cols_n),
        grid=(share,),
        in_specs=[pl.BlockSpec((devices, 1, 2, col_len, row_len), lambda h: (0, h, 0, 0, 0))],
        out_specs=pl.BlockSpec((devices, 1, col_len, row_len), lambda h: (0, h, 0, 0)),
        out_shape=jax.ShapeDtypeStruct((devices, share, col_len, row_len), jnp.bfloat16),
        scratch_shapes=[pltpu.VMEM((side, side), jnp.bfloat16)] * 2,
        name="triangle_forward",
    )(pair_ch)


def triangle_back(pair_ch, grad_ch, rows_n, cols_n):
    devices, share, _, col_len, row_len = pair_ch.shape
    side = cols_n * col_len
    return pl.pallas_call(
        functools.partial(backward_kernel, rows_n, cols_n),
        grid=(share,),
        in_specs=[
            pl.BlockSpec((devices, 1, 2, col_len, row_len), lambda h: (0, h, 0, 0, 0)),
            pl.BlockSpec((devices, 1, col_len, row_len), lambda h: (0, h, 0, 0)),
        ],
        out_specs=pl.BlockSpec((devices, 1, 2, col_len, row_len), lambda h: (0, h, 0, 0, 0)),
        out_shape=jax.ShapeDtypeStruct(pair_ch.shape, jnp.bfloat16),
        scratch_shapes=[pltpu.VMEM((side, side), jnp.bfloat16)] * 3,
        name="triangle_backward",
    )(pair_ch, grad_ch)


def total_over_all(values):
    devices = lax.axis_size(ALL)
    width = values.shape[1]
    pieces = values.reshape(devices, -1)
    arrived = lax.all_to_all(pieces, ALL, split_axis=0, concat_axis=0, tiled=True)
    own = jnp.sum(arrived, axis=0, keepdims=True)
    spread = jnp.broadcast_to(own, pieces.shape)
    return lax.all_to_all(spread, ALL, split_axis=0, concat_axis=0, tiled=True).reshape(-1, width)


def on_device(pair_rep, cotangent, lengths, weight_in, weight_out, gain_in, gain_out):
    groups = lax.axis_size("grp")
    rows_n = lax.axis_size("row")
    cols_n = lax.axis_size("col")
    devices = rows_n * cols_n
    row_len = pair_rep.shape[1]
    col_len = pair_rep.shape[2]
    hidden_width = weight_out.shape[0]
    share = hidden_width // devices
    lookup = jnp.arange(groups) == lax.axis_index("grp")
    own_length = jnp.sum(jnp.where(lookup, lengths, 0))
    row_pos = lax.axis_index("row") * row_len + jnp.arange(row_len)
    col_pos = lax.axis_index("col") * col_len + jnp.arange(col_len)
    inside = ((row_pos[:, None] < own_length) & (col_pos[None, :] < own_length)).astype(jnp.float32)
    flipped = inside.T
    inside_c = inside[:, :, None]
    z_hat, z_inverse = normalize(pair_rep[0].astype(jnp.float32), -1)
    z_norm = (z_hat * gain_in).astype(jnp.bfloat16)
    w_tri = weight_in[:, : 4 * hidden_width]
    w_gate = weight_in[:, 4 * hidden_width :]
    projected = jnp.einsum("ijc,cq->qji", z_norm, w_tri, preferred_element_type=jnp.float32)
    gate_pre = jnp.einsum("ijc,cd->ijd", z_norm, w_gate, preferred_element_type=jnp.float32)
    left_lin = projected[0:hidden_width]
    left_pre = projected[hidden_width : 2 * hidden_width]
    right_lin = projected[2 * hidden_width : 3 * hidden_width]
    right_pre = projected[3 * hidden_width :]
    left_sig = jax.nn.sigmoid(left_pre)
    right_sig = jax.nn.sigmoid(right_pre)
    pair_tiles = jnp.stack(
        [left_sig * left_lin * flipped, right_sig * right_lin * flipped], 1
    ).astype(jnp.bfloat16)
    pair_ch = exchange(pair_tiles).reshape(devices, share, 2, col_len, row_len)
    outer_ch = triangle(pair_ch, rows_n, cols_n)
    outer_tile = exchange(outer_ch.reshape(hidden_width, col_len, row_len)).astype(jnp.float32)
    o_hat, o_inverse = normalize(outer_tile, 0)
    o_norm = (o_hat * gain_out[:, None, None]).astype(jnp.bfloat16)
    proj_out = jnp.einsum("hji,hc->ijc", o_norm, weight_out, preferred_element_type=jnp.float32)
    gate = jax.nn.sigmoid(gate_pre)
    mixed = (gate * proj_out * inside_c).astype(jnp.bfloat16)
    grad_out = cotangent[0].astype(jnp.float32)
    grad_proj = (grad_out * gate * inside_c).astype(jnp.bfloat16)
    grad_gate = (grad_out * proj_out * inside_c * gate * (1.0 - gate)).astype(jnp.bfloat16)
    grad_w_out = jnp.einsum("hji,ijc->hc", o_norm, grad_proj, preferred_element_type=jnp.float32)
    grad_o_norm = jnp.einsum(
        "ijc,hc->hji", grad_proj, weight_out, preferred_element_type=jnp.float32
    )
    grad_outer = normalize_back(grad_o_norm * gain_out[:, None, None], o_hat, o_inverse, 0).astype(
        jnp.bfloat16
    )
    grad_ch = exchange(grad_outer).reshape(devices, share, col_len, row_len)
    grad_parts = triangle_back(pair_ch, grad_ch, rows_n, cols_n)
    grad_tiles = exchange(grad_parts.reshape(hidden_width, 2, col_len, row_len)).astype(jnp.float32)
    grad_left = grad_tiles[:, 0]
    grad_right = grad_tiles[:, 1]
    d_left_lin = grad_left * left_sig * flipped
    d_left_pre = grad_left * left_lin * flipped * left_sig * (1.0 - left_sig)
    d_right_lin = grad_right * right_sig * flipped
    d_right_pre = grad_right * right_lin * flipped * right_sig * (1.0 - right_sig)
    grad_proj_in = jnp.concatenate([d_left_lin, d_left_pre, d_right_lin, d_right_pre], 0).astype(
        jnp.bfloat16
    )
    grad_z_norm = jnp.einsum("qji,cq->ijc", grad_proj_in, w_tri, preferred_element_type=jnp.float32)
    grad_z_norm = grad_z_norm + jnp.einsum(
        "ijd,cd->ijc", grad_gate, w_gate, preferred_element_type=jnp.float32
    )
    grad_w_tri = jnp.einsum("ijc,qji->cq", z_norm, grad_proj_in, preferred_element_type=jnp.float32)
    grad_w_gate = jnp.einsum("ijc,ijd->cd", z_norm, grad_gate, preferred_element_type=jnp.float32)
    grad_pair = normalize_back(grad_z_norm * gain_in, z_hat, z_inverse, -1).astype(jnp.bfloat16)
    totals = total_over_all(jnp.concatenate([grad_w_tri, grad_w_gate, grad_w_out], 1)) / N
    grad_w_in = totals[:, : weight_in.shape[1]]
    grad_w_out = totals[:, weight_in.shape[1] :]
    grad_g_in = jnp.sum(grad_w_in * weight_in.astype(jnp.float32), axis=1) / gain_in
    grad_g_out = jnp.sum(grad_w_out * weight_out.astype(jnp.float32), axis=1) / gain_out
    return (mixed[None], grad_pair[None], grad_w_in, grad_w_out, grad_g_in, grad_g_out)


def solution(mesh):
    return jax.shard_map(
        on_device,
        mesh=mesh,
        in_specs=(
            P("grp", "row", "col", None),
            P("grp", "row", "col", None),
            P(),
            P(),
            P(),
            P(),
            P(),
        ),
        out_specs=(P("grp", "row", "col", None), P("grp", "row", "col", None), P(), P(), P(), P()),
        check_vma=False,
    )
```

```python
import functools

import jax
import jax.numpy as jnp
from jax import lax
from jax.experimental import pallas as pl
from jax.experimental.pallas import tpu as pltpu
from jax.sharding import PartitionSpec as P

N = 512
ALL = ("grp", "row", "col")
TILE = ("row", "col")


epsilon = 1e-05


def normalize(values, along):
    centred = values - jnp.mean(values, axis=along, keepdims=True)
    inverse = lax.rsqrt(jnp.mean(centred * centred, axis=along, keepdims=True) + epsilon)
    return (centred * inverse, inverse)


def normalize_back(grad_hat, normed, inverse, along):
    first_mean = jnp.mean(grad_hat, axis=along, keepdims=True)
    second_mean = jnp.mean(grad_hat * normed, axis=along, keepdims=True)
    return inverse * (grad_hat - first_mean - normed * second_mean)


def exchange(tiles):
    return lax.all_to_all(tiles, TILE, split_axis=0, concat_axis=0, tiled=True)


def forward_kernel(rows_n, cols_n, pair_ref, out_ref, left_ref, right_ref):
    col_len, row_len = pair_ref.shape[3], pair_ref.shape[4]
    for r in range(rows_n):
        for c in range(cols_n):
            at = (pl.ds(c * col_len, col_len), pl.ds(r * row_len, row_len))
            left_ref[at] = pair_ref[r * cols_n + c, 0, 0]
            right_ref[at] = pair_ref[r * cols_n + c, 0, 1]
    outer = lax.dot_general(
        right_ref[...], left_ref[...], (((0,), (0,)), ((), ())), preferred_element_type=jnp.float32
    ).astype(jnp.bfloat16)
    for r in range(rows_n):
        for c in range(cols_n):
            out_ref[r * cols_n + c, 0] = outer[
                c * col_len : (c + 1) * col_len, r * row_len : (r + 1) * row_len
            ]


def backward_kernel(rows_n, cols_n, pair_ref, grad_ref, out_ref, left_ref, right_ref, outer_ref):
    col_len, row_len = pair_ref.shape[3], pair_ref.shape[4]
    for r in range(rows_n):
        for c in range(cols_n):
            at = (pl.ds(c * col_len, col_len), pl.ds(r * row_len, row_len))
            left_ref[at] = pair_ref[r * cols_n + c, 0, 0]
            right_ref[at] = pair_ref[r * cols_n + c, 0, 1]
            outer_ref[at] = grad_ref[r * cols_n + c, 0]
    grad_left = lax.dot_general(
        right_ref[...], outer_ref[...], (((1,), (0,)), ((), ())), preferred_element_type=jnp.float32
    ).astype(jnp.bfloat16)
    grad_right = lax.dot_general(
        left_ref[...], outer_ref[...], (((1,), (1,)), ((), ())), preferred_element_type=jnp.float32
    ).astype(jnp.bfloat16)
    for r in range(rows_n):
        for c in range(cols_n):
            at = (slice(c * col_len, (c + 1) * col_len), slice(r * row_len, (r + 1) * row_len))
            out_ref[r * cols_n + c, 0, 0] = grad_left[at]
            out_ref[r * cols_n + c, 0, 1] = grad_right[at]


def triangle(pair_ch, rows_n, cols_n):
    devices, share, _, col_len, row_len = pair_ch.shape
    side = cols_n * col_len
    return pl.pallas_call(
        functools.partial(forward_kernel, rows_n, cols_n),
        grid=(share,),
        in_specs=[pl.BlockSpec((devices, 1, 2, col_len, row_len), lambda h: (0, h, 0, 0, 0))],
        out_specs=pl.BlockSpec((devices, 1, col_len, row_len), lambda h: (0, h, 0, 0)),
        out_shape=jax.ShapeDtypeStruct((devices, share, col_len, row_len), jnp.bfloat16),
        scratch_shapes=[pltpu.VMEM((side, side), jnp.bfloat16)] * 2,
        name="triangle_forward",
    )(pair_ch)


def triangle_back(pair_ch, grad_ch, rows_n, cols_n):
    devices, share, _, col_len, row_len = pair_ch.shape
    side = cols_n * col_len
    return pl.pallas_call(
        functools.partial(backward_kernel, rows_n, cols_n),
        grid=(share,),
        in_specs=[
            pl.BlockSpec((devices, 1, 2, col_len, row_len), lambda h: (0, h, 0, 0, 0)),
            pl.BlockSpec((devices, 1, col_len, row_len), lambda h: (0, h, 0, 0)),
        ],
        out_specs=pl.BlockSpec((devices, 1, 2, col_len, row_len), lambda h: (0, h, 0, 0, 0)),
        out_shape=jax.ShapeDtypeStruct(pair_ch.shape, jnp.bfloat16),
        scratch_shapes=[pltpu.VMEM((side, side), jnp.bfloat16)] * 3,
        name="triangle_backward",
    )(pair_ch, grad_ch)


def total_over_all(values):
    devices = lax.axis_size(ALL)
    width = values.shape[1]
    pieces = values.reshape(devices, -1)
    arrived = lax.all_to_all(pieces, ALL, split_axis=0, concat_axis=0, tiled=True)
    own = jnp.sum(arrived, axis=0, keepdims=True)
    spread = jnp.broadcast_to(own, pieces.shape)
    return lax.all_to_all(spread, ALL, split_axis=0, concat_axis=0, tiled=True).reshape(-1, width)


def project_kernel(scalar_ref, pair_ref, weight_ref, gain_ref, tile_ref, norm_ref):
    block = pl.program_id(0)
    row_len, block_len, _ = pair_ref.shape
    channels = weight_ref.shape[0] // 2
    values = jnp.swapaxes(pair_ref[...].astype(jnp.float32), 0, 1)
    normed, _ = normalize(values, -1)
    normed = (normed * gain_ref[...]).astype(jnp.bfloat16)
    norm_ref[...] = normed
    length, row_start, col_start = scalar_ref[0], scalar_ref[1], scalar_ref[2]
    row_in = row_start + lax.broadcasted_iota(jnp.int32, (1, row_len), 1) < length
    gated = []
    for j in range(block_len):
        projected = lax.dot_general(
            weight_ref[...], normed[j], (((1,), (1,)), ((), ())), preferred_element_type=jnp.float32
        )
        col_in = col_start + block * block_len + j < length
        inside = jnp.where(row_in & col_in, 1.0, 0.0)
        gated.append(projected[:channels] * jax.nn.sigmoid(projected[channels:]) * inside)
    gated = jnp.swapaxes(jnp.stack(gated, 0), 0, 1).astype(jnp.bfloat16)
    tile_ref[...] = gated.reshape(tile_ref.shape)


def project(scalars, pair_rep, weight_rows, gain, block_len=16):
    row_len, col_len, width = pair_rep.shape
    hidden_width = weight_rows.shape[0] // 4
    return pl.pallas_call(
        project_kernel,
        grid=(col_len // block_len,),
        in_specs=[
            pl.BlockSpec(memory_space=pltpu.SMEM),
            pl.BlockSpec((row_len, block_len, width), lambda j: (0, j, 0)),
            pl.BlockSpec(weight_rows.shape, lambda j: (0, 0)),
            pl.BlockSpec((1, width), lambda j: (0, 0)),
        ],
        out_specs=[
            pl.BlockSpec((hidden_width, 2, block_len, row_len), lambda j: (0, 0, j, 0)),
            pl.BlockSpec((block_len, row_len, width), lambda j: (j, 0, 0)),
        ],
        out_shape=[
            jax.ShapeDtypeStruct((hidden_width, 2, col_len, row_len), jnp.bfloat16),
            jax.ShapeDtypeStruct((col_len, row_len, width), jnp.bfloat16),
        ],
        name="project",
    )(scalars, pair_rep, weight_rows, gain[None])


def outer_grad_kernel(outer_ref, back_ref, mean_ref, grad_ref):
    o_hat, o_inverse = normalize(outer_ref[...].astype(jnp.float32), 0)
    back = back_ref[...]
    second_mean = jnp.mean(back * o_hat, axis=0, keepdims=True)
    grad = o_inverse * (back - mean_ref[...][None] - o_hat * second_mean)
    grad_ref[...] = grad.astype(jnp.bfloat16)


def outer_grad(outer_tile, back, back_mean, block_len=16):
    hidden_width, col_len, row_len = outer_tile.shape
    whole = pl.BlockSpec((hidden_width, block_len, row_len), lambda j: (0, j, 0))
    return pl.pallas_call(
        outer_grad_kernel,
        grid=(col_len // block_len,),
        in_specs=[whole, whole, pl.BlockSpec((block_len, row_len), lambda j: (j, 0))],
        out_specs=whole,
        out_shape=jax.ShapeDtypeStruct(outer_tile.shape, jnp.bfloat16),
        name="outer_grad",
    )(outer_tile, back, back_mean)


def on_device(pair_rep, cotangent, lengths, weight_in, weight_out, gain_in, gain_out):
    groups = lax.axis_size("grp")
    rows_n = lax.axis_size("row")
    cols_n = lax.axis_size("col")
    devices = rows_n * cols_n
    row_len = pair_rep.shape[1]
    col_len = pair_rep.shape[2]
    width = pair_rep.shape[3]
    hidden_width = weight_out.shape[0]
    share = hidden_width // devices
    lookup = jnp.arange(groups) == lax.axis_index("grp")
    own_length = jnp.sum(jnp.where(lookup, lengths, 0))
    row_start = lax.axis_index("row") * row_len
    col_start = lax.axis_index("col") * col_len
    scalars = jnp.stack([own_length, row_start, col_start]).astype(jnp.int32)
    row_in = row_start + jnp.arange(row_len) < own_length
    col_in = col_start + jnp.arange(col_len) < own_length
    flipped = (col_in[:, None] & row_in[None, :]).astype(jnp.float32)
    flipped_c = flipped[:, :, None]
    w_gate = weight_in[:, 4 * hidden_width :]
    w_tri = weight_in[:, : 4 * hidden_width].reshape(width, 2, 2, hidden_width)
    w_tri = w_tri.transpose(0, 2, 3, 1).reshape(width, 4 * hidden_width)

    pair_tiles, z_norm = project(scalars, pair_rep[0], w_tri.T, gain_in)
    pair_ch = exchange(pair_tiles).reshape(devices, share, 2, col_len, row_len)

    projected = jnp.einsum("jic,cq->qji", z_norm, w_tri, preferred_element_type=jnp.float32)
    projected = projected.reshape(2, hidden_width, 2, col_len, row_len)
    sig = jax.nn.sigmoid(projected[1])
    factors = jnp.stack([sig * flipped, projected[0] * flipped * sig * (1.0 - sig)], 0)
    factors = factors.astype(jnp.bfloat16)
    gate_pre = jnp.einsum("jic,cd->jid", z_norm, w_gate, preferred_element_type=jnp.float32)
    gate = jax.nn.sigmoid(gate_pre) * flipped_c
    grad_out = jnp.swapaxes(cotangent[0], 0, 1).astype(jnp.float32)
    grad_proj = (grad_out * gate).astype(jnp.bfloat16)
    grad_o_norm = jnp.einsum(
        "jic,hc->hji", grad_proj, weight_out, preferred_element_type=jnp.float32
    )
    back = grad_o_norm * gain_out[:, None, None]
    back_mean = jnp.mean(back, axis=0)
    pair_ch, factors, gate, grad_proj, back, back_mean = lax.optimization_barrier(
        (pair_ch, factors, gate, grad_proj, back, back_mean)
    )

    outer_ch = triangle(pair_ch, rows_n, cols_n)
    outer_tile = exchange(outer_ch.reshape(hidden_width, col_len, row_len))
    grad_outer = outer_grad(outer_tile, back, back_mean)
    grad_ch = exchange(grad_outer).reshape(devices, share, col_len, row_len)

    o_hat, _ = normalize(outer_tile.astype(jnp.float32), 0)
    o_norm = (o_hat * gain_out[:, None, None]).astype(jnp.bfloat16)
    proj_out = jnp.einsum("hji,hc->jic", o_norm, weight_out, preferred_element_type=jnp.float32)
    mixed = jnp.swapaxes((gate * proj_out).astype(jnp.bfloat16), 0, 1)
    grad_gate = (grad_out * proj_out * gate * (1.0 - gate)).astype(jnp.bfloat16)
    grad_w_out = jnp.einsum("hji,jic->hc", o_norm, grad_proj, preferred_element_type=jnp.float32)
    grad_w_gate = jnp.einsum("jic,jid->cd", z_norm, grad_gate, preferred_element_type=jnp.float32)
    grad_z_gate = jnp.einsum("jid,cd->jic", grad_gate, w_gate, preferred_element_type=jnp.float32)

    grad_ch, mixed, grad_z_gate, grad_w_gate, grad_w_out = lax.optimization_barrier(
        (grad_ch, mixed, grad_z_gate, grad_w_gate, grad_w_out)
    )
    grad_parts = triangle_back(pair_ch, grad_ch, rows_n, cols_n)
    grad_tiles = exchange(grad_parts.reshape(hidden_width, 2, col_len, row_len))
    grad_proj_in = (grad_tiles.astype(jnp.float32) * factors.astype(jnp.float32)).astype(jnp.bfloat16)
    grad_proj_in = grad_proj_in.reshape(4 * hidden_width, col_len, row_len)
    grad_w_tri = jnp.einsum("jic,qji->cq", z_norm, grad_proj_in, preferred_element_type=jnp.float32)
    totals = total_over_all(jnp.concatenate([grad_w_tri, grad_w_gate, grad_w_out], 1)) / N
    grad_w_tri = totals[:, : 4 * hidden_width].reshape(width, 2, hidden_width, 2)
    grad_w_tri = grad_w_tri.transpose(0, 3, 1, 2).reshape(width, 4 * hidden_width)
    grad_w_in = jnp.concatenate(
        [grad_w_tri, totals[:, 4 * hidden_width : weight_in.shape[1]]], 1
    )
    grad_w_out = totals[:, weight_in.shape[1] :]
    grad_g_in = jnp.sum(grad_w_in * weight_in.astype(jnp.float32), axis=1) / gain_in
    grad_g_out = jnp.sum(grad_w_out * weight_out.astype(jnp.float32), axis=1) / gain_out

    z_hat, z_inverse = normalize(jnp.swapaxes(pair_rep[0], 0, 1).astype(jnp.float32), -1)
    grad_z_norm = grad_z_gate + jnp.einsum(
        "qji,cq->jic", grad_proj_in, w_tri, preferred_element_type=jnp.float32
    )
    grad_pair = normalize_back(grad_z_norm * gain_in, z_hat, z_inverse, -1)
    grad_pair = jnp.swapaxes(grad_pair.astype(jnp.bfloat16), 0, 1)
    return (mixed[None], grad_pair[None], grad_w_in, grad_w_out, grad_g_in, grad_g_out)


def solution(mesh):
    return jax.shard_map(
        on_device,
        mesh=mesh,
        in_specs=(
            P("grp", "row", "col", None),
            P("grp", "row", "col", None),
            P(),
            P(),
            P(),
            P(),
            P(),
        ),
        out_specs=(P("grp", "row", "col", None), P("grp", "row", "col", None), P(), P(), P(), P()),
        check_vma=False,
    )
```

```python
import functools

import jax
import jax.numpy as jnp
from jax import lax
from jax.experimental import pallas as pl
from jax.experimental.pallas import tpu as pltpu
from jax.sharding import PartitionSpec as P

N = 512
ALL = ("grp", "row", "col")
TILE = ("row", "col")


epsilon = 1e-05


def normalize(values, along):
    centred = values - jnp.mean(values, axis=along, keepdims=True)
    inverse = lax.rsqrt(jnp.mean(centred * centred, axis=along, keepdims=True) + epsilon)
    return (centred * inverse, inverse)


def normalize_back(grad_hat, normed, inverse, along):
    first_mean = jnp.mean(grad_hat, axis=along, keepdims=True)
    second_mean = jnp.mean(grad_hat * normed, axis=along, keepdims=True)
    return inverse * (grad_hat - first_mean - normed * second_mean)


def exchange(tiles):
    return lax.all_to_all(tiles, TILE, split_axis=0, concat_axis=0, tiled=True)


def forward_kernel(rows_n, cols_n, pair_ref, out_ref, left_ref, right_ref):
    col_len, row_len = pair_ref.shape[3], pair_ref.shape[4]
    for r in range(rows_n):
        for c in range(cols_n):
            at = (pl.ds(c * col_len, col_len), pl.ds(r * row_len, row_len))
            left_ref[at] = pair_ref[r * cols_n + c, 0, 0]
            right_ref[at] = pair_ref[r * cols_n + c, 0, 1]
    outer = lax.dot_general(
        right_ref[...], left_ref[...], (((0,), (0,)), ((), ())), preferred_element_type=jnp.float32
    ).astype(jnp.bfloat16)
    for r in range(rows_n):
        for c in range(cols_n):
            out_ref[r * cols_n + c, 0] = outer[
                c * col_len : (c + 1) * col_len, r * row_len : (r + 1) * row_len
            ]


def backward_kernel(rows_n, cols_n, pair_ref, grad_ref, out_ref, left_ref, right_ref, outer_ref):
    col_len, row_len = pair_ref.shape[3], pair_ref.shape[4]
    for r in range(rows_n):
        for c in range(cols_n):
            at = (pl.ds(c * col_len, col_len), pl.ds(r * row_len, row_len))
            left_ref[at] = pair_ref[r * cols_n + c, 0, 0]
            right_ref[at] = pair_ref[r * cols_n + c, 0, 1]
            outer_ref[at] = grad_ref[r * cols_n + c, 0]
    grad_left = lax.dot_general(
        right_ref[...], outer_ref[...], (((1,), (0,)), ((), ())), preferred_element_type=jnp.float32
    ).astype(jnp.bfloat16)
    grad_right = lax.dot_general(
        left_ref[...], outer_ref[...], (((1,), (1,)), ((), ())), preferred_element_type=jnp.float32
    ).astype(jnp.bfloat16)
    for r in range(rows_n):
        for c in range(cols_n):
            at = (slice(c * col_len, (c + 1) * col_len), slice(r * row_len, (r + 1) * row_len))
            out_ref[r * cols_n + c, 0, 0] = grad_left[at]
            out_ref[r * cols_n + c, 0, 1] = grad_right[at]


def triangle(pair_ch, rows_n, cols_n):
    devices, share, _, col_len, row_len = pair_ch.shape
    side = cols_n * col_len
    return pl.pallas_call(
        functools.partial(forward_kernel, rows_n, cols_n),
        grid=(share,),
        in_specs=[pl.BlockSpec((devices, 1, 2, col_len, row_len), lambda h: (0, h, 0, 0, 0))],
        out_specs=pl.BlockSpec((devices, 1, col_len, row_len), lambda h: (0, h, 0, 0)),
        out_shape=jax.ShapeDtypeStruct((devices, share, col_len, row_len), jnp.bfloat16),
        scratch_shapes=[pltpu.VMEM((side, side), jnp.bfloat16)] * 2,
        name="triangle_forward",
    )(pair_ch)


def triangle_back(pair_ch, grad_ch, rows_n, cols_n):
    devices, share, _, col_len, row_len = pair_ch.shape
    side = cols_n * col_len
    return pl.pallas_call(
        functools.partial(backward_kernel, rows_n, cols_n),
        grid=(share,),
        in_specs=[
            pl.BlockSpec((devices, 1, 2, col_len, row_len), lambda h: (0, h, 0, 0, 0)),
            pl.BlockSpec((devices, 1, col_len, row_len), lambda h: (0, h, 0, 0)),
        ],
        out_specs=pl.BlockSpec((devices, 1, 2, col_len, row_len), lambda h: (0, h, 0, 0, 0)),
        out_shape=jax.ShapeDtypeStruct(pair_ch.shape, jnp.bfloat16),
        scratch_shapes=[pltpu.VMEM((side, side), jnp.bfloat16)] * 3,
        name="triangle_backward",
    )(pair_ch, grad_ch)


def total_over_all(values):
    devices = lax.axis_size(ALL)
    pieces = values.reshape(devices, -1, values.shape[1])
    arrived = lax.all_to_all(pieces, ALL, split_axis=0, concat_axis=0, tiled=True)
    spread = jnp.broadcast_to(jnp.sum(arrived, axis=0, keepdims=True), pieces.shape)
    return lax.all_to_all(spread, ALL, split_axis=0, concat_axis=0, tiled=True).reshape(values.shape)


def layer_norm(values):
    centred = values - jnp.mean(values, axis=-1, keepdims=True)
    inverse = lax.rsqrt(jnp.mean(centred * centred, axis=-1, keepdims=True) + epsilon)
    return centred * inverse, inverse


def tile_inside(lengths_ref, row_len, block_len):
    length = lengths_ref[lax.axis_index("grp")]
    row_start = lax.axis_index("row") * row_len
    col_start = (lax.axis_index("col") * pl.num_programs(0) + pl.program_id(0)) * block_len
    row_in = row_start + lax.broadcasted_iota(jnp.int32, (1, row_len), 1) < length
    return [
        jnp.where(row_in & (col_start + j < length), 1.0, 0.0).astype(jnp.float32)
        for j in range(block_len)
    ]


def project_kernel(lengths_ref, pair_ref, weight_ref, gain_ref, tile_ref, norm_ref, rows_ref):
    row_len, block_len, _ = pair_ref.shape
    hidden_width = tile_ref.shape[0]

    @pl.when(pl.program_id(0) == 0)
    def _():
        for at, source in enumerate((0, 2, 1, 3)):
            part = weight_ref[:, source * hidden_width : (source + 1) * hidden_width]
            rows_ref[at * hidden_width : (at + 1) * hidden_width] = part.astype(jnp.float32).T.astype(
                jnp.bfloat16
            )

    normed, _ = layer_norm(jnp.swapaxes(pair_ref[...].astype(jnp.float32), 0, 1))
    normed = (normed * gain_ref[...]).astype(jnp.bfloat16)
    norm_ref[...] = normed
    inside = tile_inside(lengths_ref, row_len, block_len)
    gated = []
    for j in range(block_len):
        projected = lax.dot_general(
            rows_ref[...], normed[j], (((1,), (1,)), ((), ())), preferred_element_type=jnp.float32
        )
        sig = jax.nn.sigmoid(projected[2 * hidden_width :])
        gated.append(projected[: 2 * hidden_width] * sig * inside[j])
    gated = jnp.swapaxes(jnp.stack(gated, 0), 0, 1).astype(jnp.bfloat16)
    tile_ref[:, 0] = gated[:hidden_width]
    tile_ref[:, 1] = gated[hidden_width:]


def project(lengths, pair_rep, weight_in, gain, block_len=16):
    row_len, col_len, width = pair_rep.shape
    hidden_width = (weight_in.shape[1] - width) // 4
    return pl.pallas_call(
        project_kernel,
        grid=(col_len // block_len,),
        in_specs=[
            pl.BlockSpec(memory_space=pltpu.SMEM),
            pl.BlockSpec((row_len, block_len, width), lambda j: (0, j, 0)),
            pl.BlockSpec(weight_in.shape, lambda j: (0, 0)),
            pl.BlockSpec((1, width), lambda j: (0, 0)),
        ],
        out_specs=[
            pl.BlockSpec((hidden_width, 2, block_len, row_len), lambda j: (0, 0, j, 0)),
            pl.BlockSpec((block_len, row_len, width), lambda j: (j, 0, 0)),
        ],
        out_shape=[
            jax.ShapeDtypeStruct((hidden_width, 2, col_len, row_len), jnp.bfloat16),
            jax.ShapeDtypeStruct((col_len, row_len, width), jnp.bfloat16),
        ],
        scratch_shapes=[pltpu.VMEM((4 * hidden_width, width), jnp.bfloat16)],
        name="project",
    )(lengths, pair_rep, weight_in, gain[None])


def factors_kernel(lengths_ref, norm_ref, weight_ref, factor_ref):
    block_len, row_len, _ = norm_ref.shape
    half = weight_ref.shape[0] // 2
    inside = tile_inside(lengths_ref, row_len, block_len)
    for j in range(block_len):
        projected = lax.dot_general(
            weight_ref[...], norm_ref[j], (((1,), (1,)), ((), ())), preferred_element_type=jnp.float32
        )
        sig = jax.nn.sigmoid(projected[half:])
        kept = sig * inside[j]
        factor_ref[j, :half] = kept.astype(jnp.bfloat16)
        factor_ref[j, half:] = (projected[:half] * kept * (1.0 - sig)).astype(jnp.bfloat16)


def gate_factors(lengths, z_norm, weight_rows, block_len=16):
    col_len, row_len, width = z_norm.shape
    return pl.pallas_call(
        factors_kernel,
        grid=(col_len // block_len,),
        in_specs=[
            pl.BlockSpec(memory_space=pltpu.SMEM),
            pl.BlockSpec((block_len, row_len, width), lambda j: (j, 0, 0)),
            pl.BlockSpec(weight_rows.shape, lambda j: (0, 0)),
        ],
        out_specs=pl.BlockSpec((block_len, weight_rows.shape[0], row_len), lambda j: (j, 0, 0)),
        out_shape=jax.ShapeDtypeStruct((col_len, weight_rows.shape[0], row_len), jnp.bfloat16),
        name="gate_factors",
    )(lengths, z_norm, weight_rows)


def projection_grads(grad_ref, factor_ref):
    hidden_width, _, block_len, row_len = grad_ref.shape
    grads = grad_ref[...].astype(jnp.float32).reshape(2 * hidden_width, block_len, row_len)
    grads = jnp.swapaxes(grads, 0, 1)
    return [
        jnp.concatenate(
            [
                (grads[j] * factor_ref[j, : 2 * hidden_width].astype(jnp.float32)),
                (grads[j] * factor_ref[j, 2 * hidden_width :].astype(jnp.float32)),
            ],
            0,
        ).astype(jnp.bfloat16)
        for j in range(block_len)
    ]


def weight_sums_kernel(grad_ref, factor_ref, norm_ref, gate_ref, out_ref, sum_ref, total_ref):
    hidden_width, _, block_len, row_len = grad_ref.shape
    width = norm_ref.shape[2]
    step = pl.program_id(0)
    grads = jnp.concatenate(projection_grads(grad_ref, factor_ref), 1)
    partial = jnp.dot(
        grads,
        norm_ref[...].reshape(block_len * row_len, width),
        preferred_element_type=jnp.float32,
    )

    @pl.when(step == 0)
    def _():
        total_ref[...] = partial

    @pl.when(step > 0)
    def _():
        total_ref[...] += partial

    @pl.when(step == pl.num_programs(0) - 1)
    def _():
        for side in range(2):
            for kind in range(2):
                rows = total_ref[
                    pl.ds(kind * 2 * hidden_width + side, hidden_width, stride=2), :
                ]
                at = (2 * side + kind) * width
                sum_ref[at : at + width] = rows.T
        sum_ref[4 * width : 5 * width] = gate_ref[...]
        sum_ref[5 * width : 6 * width] = out_ref[...]
        sum_ref[6 * width :] = jnp.zeros((2 * width, width), jnp.float32)


def weight_sums(grad_tiles, factors, z_norm, grad_w_gate, grad_w_out, block_len=16):
    hidden_width, _, col_len, row_len = grad_tiles.shape
    width = z_norm.shape[2]
    square = pl.BlockSpec((width, width), lambda j: (0, 0))
    return pl.pallas_call(
        weight_sums_kernel,
        grid=(col_len // block_len,),
        in_specs=[
            pl.BlockSpec((hidden_width, 2, block_len, row_len), lambda j: (0, 0, j, 0)),
            pl.BlockSpec((block_len, 4 * hidden_width, row_len), lambda j: (j, 0, 0)),
            pl.BlockSpec((block_len, row_len, width), lambda j: (j, 0, 0)),
            square,
            square,
        ],
        out_specs=pl.BlockSpec((8 * width, width), lambda j: (0, 0)),
        out_shape=jax.ShapeDtypeStruct((8 * width, width), jnp.float32),
        scratch_shapes=[pltpu.VMEM((4 * hidden_width, width), jnp.float32)],
        name="weight_sums",
    )(grad_tiles, factors, z_norm, grad_w_gate, grad_w_out)


def pair_grad_kernel(
    pair_ref, grad_ref, factor_ref, gate_ref, weight_ref, w_gate_ref, gain_ref, out_ref
):
    block_len = pair_ref.shape[1]
    z_hat, z_inverse = layer_norm(jnp.swapaxes(pair_ref[...].astype(jnp.float32), 0, 1))
    grads = projection_grads(grad_ref, factor_ref)
    grad_norm = []
    for j in range(block_len):
        total = jnp.dot(weight_ref[...], grads[j], preferred_element_type=jnp.float32)
        total += lax.dot_general(
            w_gate_ref[...], gate_ref[j], (((1,), (1,)), ((), ())), preferred_element_type=jnp.float32
        )
        grad_norm.append(total.T)
    grad_hat = jnp.stack(grad_norm, 0) * gain_ref[...]
    grad_pair = normalize_back(grad_hat, z_hat, z_inverse, -1)
    out_ref[...] = jnp.swapaxes(grad_pair, 0, 1).astype(jnp.bfloat16)


def pair_grad(pair_rep, grad_tiles, factors, grad_gate, w_tri, w_gate, gain, block_len=16):
    row_len, col_len, width = pair_rep.shape
    hidden_width = grad_tiles.shape[0]
    return pl.pallas_call(
        pair_grad_kernel,
        grid=(col_len // block_len,),
        in_specs=[
            pl.BlockSpec((row_len, block_len, width), lambda j: (0, j, 0)),
            pl.BlockSpec((hidden_width, 2, block_len, row_len), lambda j: (0, 0, j, 0)),
            pl.BlockSpec((block_len, 4 * hidden_width, row_len), lambda j: (j, 0, 0)),
            pl.BlockSpec((block_len, row_len, width), lambda j: (j, 0, 0)),
            pl.BlockSpec(w_tri.shape, lambda j: (0, 0)),
            pl.BlockSpec(w_gate.shape, lambda j: (0, 0)),
            pl.BlockSpec((1, width), lambda j: (0, 0)),
        ],
        out_specs=pl.BlockSpec((row_len, block_len, width), lambda j: (0, j, 0)),
        out_shape=jax.ShapeDtypeStruct(pair_rep.shape, jnp.bfloat16),
        name="pair_grad",
    )(pair_rep, grad_tiles, factors, grad_gate, w_tri, w_gate, gain[None])


def outer_grad_kernel(outer_ref, back_ref, mean_ref, grad_ref):
    o_hat, o_inverse = normalize(outer_ref[...].astype(jnp.float32), 0)
    back = back_ref[...]
    second_mean = jnp.mean(back * o_hat, axis=0, keepdims=True)
    grad = o_inverse * (back - mean_ref[...][None] - o_hat * second_mean)
    grad_ref[...] = grad.astype(jnp.bfloat16)


def outer_grad(outer_tile, back, back_mean, block_len=16):
    hidden_width, col_len, row_len = outer_tile.shape
    whole = pl.BlockSpec((hidden_width, block_len, row_len), lambda j: (0, j, 0))
    return pl.pallas_call(
        outer_grad_kernel,
        grid=(col_len // block_len,),
        in_specs=[whole, whole, pl.BlockSpec((block_len, row_len), lambda j: (j, 0))],
        out_specs=whole,
        out_shape=jax.ShapeDtypeStruct(outer_tile.shape, jnp.bfloat16),
        name="outer_grad",
    )(outer_tile, back, back_mean)


def on_device(pair_rep, cotangent, lengths, weight_in, weight_out, gain_in, gain_out):
    groups = lax.axis_size("grp")
    rows_n = lax.axis_size("row")
    cols_n = lax.axis_size("col")
    devices = rows_n * cols_n
    row_len = pair_rep.shape[1]
    col_len = pair_rep.shape[2]
    width = pair_rep.shape[3]
    hidden_width = weight_out.shape[0]
    share = hidden_width // devices
    lookup = jnp.arange(groups) == lax.axis_index("grp")
    own_length = jnp.sum(jnp.where(lookup, lengths, 0))
    row_in = lax.axis_index("row") * row_len + jnp.arange(row_len) < own_length
    col_in = lax.axis_index("col") * col_len + jnp.arange(col_len) < own_length
    flipped_c = (col_in[:, None] & row_in[None, :]).astype(jnp.float32)[:, :, None]
    w_gate = weight_in[:, 4 * hidden_width :]

    pair_tiles, z_norm = project(lengths, pair_rep[0], weight_in, gain_in)
    pair_ch = exchange(pair_tiles).reshape(devices, share, 2, col_len, row_len)

    w_tri = weight_in[:, : 4 * hidden_width].reshape(width, 2, 2, hidden_width)
    w_tri = w_tri.transpose(0, 2, 3, 1).reshape(width, 4 * hidden_width)
    factors = gate_factors(lengths, z_norm, w_tri.T)
    gate_pre = jnp.einsum("jic,cd->jid", z_norm, w_gate, preferred_element_type=jnp.float32)
    gate = jax.nn.sigmoid(gate_pre) * flipped_c
    grad_out = jnp.swapaxes(cotangent[0], 0, 1).astype(jnp.float32)
    grad_proj = (grad_out * gate).astype(jnp.bfloat16)
    grad_o_norm = jnp.einsum(
        "jic,hc->hji", grad_proj, weight_out, preferred_element_type=jnp.float32
    )
    back = grad_o_norm * gain_out[:, None, None]
    back_mean = jnp.mean(back, axis=0)
    pair_ch, factors, gate, grad_proj, back, back_mean = lax.optimization_barrier(
        (pair_ch, factors, gate, grad_proj, back, back_mean)
    )

    outer_ch = triangle(pair_ch, rows_n, cols_n)
    outer_tile = exchange(outer_ch.reshape(hidden_width, col_len, row_len))
    grad_outer = outer_grad(outer_tile, back, back_mean)
    grad_ch = exchange(grad_outer).reshape(devices, share, col_len, row_len)

    o_hat, _ = normalize(outer_tile.astype(jnp.float32), 0)
    o_norm = (o_hat * gain_out[:, None, None]).astype(jnp.bfloat16)
    proj_out = jnp.einsum("hji,hc->jic", o_norm, weight_out, preferred_element_type=jnp.float32)
    mixed = jnp.swapaxes((gate * proj_out).astype(jnp.bfloat16), 0, 1)
    grad_gate = (grad_out * proj_out * gate * (1.0 - gate)).astype(jnp.bfloat16)
    grad_w_out = jnp.einsum("hji,jic->hc", o_norm, grad_proj, preferred_element_type=jnp.float32)
    grad_w_gate = jnp.einsum("jic,jid->cd", z_norm, grad_gate, preferred_element_type=jnp.float32)

    grad_ch, mixed, grad_gate, grad_w_gate, grad_w_out = lax.optimization_barrier(
        (grad_ch, mixed, grad_gate, grad_w_gate, grad_w_out)
    )
    grad_parts = triangle_back(pair_ch, grad_ch, rows_n, cols_n)
    grad_tiles = exchange(grad_parts.reshape(hidden_width, 2, col_len, row_len))
    sums = weight_sums(grad_tiles, factors, z_norm, grad_w_gate, grad_w_out)
    totals = total_over_all(sums).reshape(8, width, width) / N
    grad_w_in = jnp.concatenate([totals[block] for block in range(5)], 1)
    grad_w_out = totals[5]
    grad_g_in = jnp.sum(grad_w_in * weight_in.astype(jnp.float32), axis=1) / gain_in
    grad_g_out = jnp.sum(grad_w_out * weight_out.astype(jnp.float32), axis=1) / gain_out
    grad_pair = pair_grad(pair_rep[0], grad_tiles, factors, grad_gate, w_tri, w_gate, gain_in)
    return (mixed[None], grad_pair[None], grad_w_in, grad_w_out, grad_g_in, grad_g_out)


def solution(mesh):
    return jax.shard_map(
        on_device,
        mesh=mesh,
        in_specs=(
            P("grp", "row", "col", None),
            P("grp", "row", "col", None),
            P(),
            P(),
            P(),
            P(),
            P(),
        ),
        out_specs=(P("grp", "row", "col", None), P("grp", "row", "col", None), P(), P(), P(), P()),
        check_vma=False,
    )
```

```python
import functools

import jax
import jax.numpy as jnp
from jax import lax
from jax.experimental import pallas as pl
from jax.experimental.pallas import tpu as pltpu
from jax.sharding import PartitionSpec as P

N = 512
ALL = ("grp", "row", "col")
TILE = ("row", "col")
STAGGER_NS = 22000


epsilon = 1e-05


def normalize(values, along):
    centred = values - jnp.mean(values, axis=along, keepdims=True)
    inverse = lax.rsqrt(jnp.mean(centred * centred, axis=along, keepdims=True) + epsilon)
    return (centred * inverse, inverse)


def normalize_back(grad_hat, normed, inverse, along):
    first_mean = jnp.mean(grad_hat, axis=along, keepdims=True)
    second_mean = jnp.mean(grad_hat * normed, axis=along, keepdims=True)
    return inverse * (grad_hat - first_mean - normed * second_mean)


def exchange(tiles):
    return lax.all_to_all(tiles, TILE, split_axis=0, concat_axis=0, tiled=True)


def forward_kernel(rows_n, cols_n, pair_ref, out_ref, left_ref, right_ref):
    col_len, row_len = pair_ref.shape[3], pair_ref.shape[4]
    for r in range(rows_n):
        for c in range(cols_n):
            at = (pl.ds(c * col_len, col_len), pl.ds(r * row_len, row_len))
            left_ref[at] = pair_ref[r * cols_n + c, 0, 0]
            right_ref[at] = pair_ref[r * cols_n + c, 0, 1]
    outer = lax.dot_general(
        right_ref[...], left_ref[...], (((0,), (0,)), ((), ())), preferred_element_type=jnp.float32
    ).astype(jnp.bfloat16)
    for r in range(rows_n):
        for c in range(cols_n):
            out_ref[r * cols_n + c, 0] = outer[
                c * col_len : (c + 1) * col_len, r * row_len : (r + 1) * row_len
            ]


def backward_kernel(rows_n, cols_n, pair_ref, grad_ref, out_ref, left_ref, right_ref, outer_ref):
    col_len, row_len = pair_ref.shape[3], pair_ref.shape[4]
    for r in range(rows_n):
        for c in range(cols_n):
            at = (pl.ds(c * col_len, col_len), pl.ds(r * row_len, row_len))
            left_ref[at] = pair_ref[r * cols_n + c, 0, 0]
            right_ref[at] = pair_ref[r * cols_n + c, 0, 1]
            outer_ref[at] = grad_ref[r * cols_n + c, 0]
    grad_left = lax.dot_general(
        right_ref[...], outer_ref[...], (((1,), (0,)), ((), ())), preferred_element_type=jnp.float32
    ).astype(jnp.bfloat16)
    grad_right = lax.dot_general(
        left_ref[...], outer_ref[...], (((1,), (1,)), ((), ())), preferred_element_type=jnp.float32
    ).astype(jnp.bfloat16)
    for r in range(rows_n):
        for c in range(cols_n):
            at = (slice(c * col_len, (c + 1) * col_len), slice(r * row_len, (r + 1) * row_len))
            out_ref[r * cols_n + c, 0, 0] = grad_left[at]
            out_ref[r * cols_n + c, 0, 1] = grad_right[at]


def triangle(pair_ch, rows_n, cols_n):
    devices, share, _, col_len, row_len = pair_ch.shape
    side = cols_n * col_len
    return pl.pallas_call(
        functools.partial(forward_kernel, rows_n, cols_n),
        grid=(share,),
        in_specs=[pl.BlockSpec((devices, 1, 2, col_len, row_len), lambda h: (0, h, 0, 0, 0))],
        out_specs=pl.BlockSpec((devices, 1, col_len, row_len), lambda h: (0, h, 0, 0)),
        out_shape=jax.ShapeDtypeStruct((devices, share, col_len, row_len), jnp.bfloat16),
        scratch_shapes=[pltpu.VMEM((side, side), jnp.bfloat16)] * 2,
        name="triangle_forward",
    )(pair_ch)


def triangle_back(pair_ch, grad_ch, rows_n, cols_n):
    devices, share, _, col_len, row_len = pair_ch.shape
    side = cols_n * col_len
    return pl.pallas_call(
        functools.partial(backward_kernel, rows_n, cols_n),
        grid=(share,),
        in_specs=[
            pl.BlockSpec((devices, 1, 2, col_len, row_len), lambda h: (0, h, 0, 0, 0)),
            pl.BlockSpec((devices, 1, col_len, row_len), lambda h: (0, h, 0, 0)),
        ],
        out_specs=pl.BlockSpec((devices, 1, 2, col_len, row_len), lambda h: (0, h, 0, 0, 0)),
        out_shape=jax.ShapeDtypeStruct(pair_ch.shape, jnp.bfloat16),
        scratch_shapes=[pltpu.VMEM((side, side), jnp.bfloat16)] * 3,
        name="triangle_backward",
    )(pair_ch, grad_ch)


def layer_norm(values):
    centred = values - jnp.mean(values, axis=-1, keepdims=True)
    inverse = lax.rsqrt(jnp.mean(centred * centred, axis=-1, keepdims=True) + epsilon)
    return centred * inverse, inverse


def tile_inside(lengths_ref, row_len, block_len):
    length = lengths_ref[lax.axis_index("grp")]
    row_start = lax.axis_index("row") * row_len
    col_start = (lax.axis_index("col") * pl.num_programs(0) + pl.program_id(0)) * block_len
    row_in = row_start + lax.broadcasted_iota(jnp.int32, (1, row_len), 1) < length
    return [
        jnp.where(row_in & (col_start + j < length), 1.0, 0.0).astype(jnp.float32)
        for j in range(block_len)
    ]


def project_kernel(lengths_ref, pair_ref, weight_ref, gain_ref, tile_ref, norm_ref, rows_ref):
    row_len, block_len, _ = pair_ref.shape
    hidden_width = tile_ref.shape[0]
    first = pl.program_id(0) == 0

    @pl.when(first & (lax.axis_index("grp") % 2 == 1))
    def _():
        pl.delay(STAGGER_NS)

    @pl.when(first)
    def _():
        for at, source in enumerate((0, 2, 1, 3)):
            part = weight_ref[:, source * hidden_width : (source + 1) * hidden_width]
            rows_ref[at * hidden_width : (at + 1) * hidden_width] = part.astype(jnp.float32).T.astype(
                jnp.bfloat16
            )

    normed, _ = layer_norm(jnp.swapaxes(pair_ref[...].astype(jnp.float32), 0, 1))
    normed = (normed * gain_ref[...]).astype(jnp.bfloat16)
    norm_ref[...] = normed
    inside = tile_inside(lengths_ref, row_len, block_len)
    gated = []
    for j in range(block_len):
        projected = lax.dot_general(
            rows_ref[...], normed[j], (((1,), (1,)), ((), ())), preferred_element_type=jnp.float32
        )
        sig = jax.nn.sigmoid(projected[2 * hidden_width :])
        gated.append(projected[: 2 * hidden_width] * sig * inside[j])
    gated = jnp.swapaxes(jnp.stack(gated, 0), 0, 1).astype(jnp.bfloat16)
    tile_ref[:, 0] = gated[:hidden_width]
    tile_ref[:, 1] = gated[hidden_width:]


def project(lengths, pair_rep, weight_in, gain, block_len=16):
    row_len, col_len, width = pair_rep.shape
    hidden_width = (weight_in.shape[1] - width) // 4
    return pl.pallas_call(
        project_kernel,
        grid=(col_len // block_len,),
        in_specs=[
            pl.BlockSpec(memory_space=pltpu.SMEM),
            pl.BlockSpec((row_len, block_len, width), lambda j: (0, j, 0)),
            pl.BlockSpec(weight_in.shape, lambda j: (0, 0)),
            pl.BlockSpec((1, width), lambda j: (0, 0)),
        ],
        out_specs=[
            pl.BlockSpec((hidden_width, 2, block_len, row_len), lambda j: (0, 0, j, 0)),
            pl.BlockSpec((block_len, row_len, width), lambda j: (j, 0, 0)),
        ],
        out_shape=[
            jax.ShapeDtypeStruct((hidden_width, 2, col_len, row_len), jnp.bfloat16),
            jax.ShapeDtypeStruct((col_len, row_len, width), jnp.bfloat16),
        ],
        scratch_shapes=[pltpu.VMEM((4 * hidden_width, width), jnp.bfloat16)],
        name="project",
    )(lengths, pair_rep, weight_in, gain[None])


def factors_kernel(lengths_ref, norm_ref, weight_ref, factor_ref):
    block_len, row_len, _ = norm_ref.shape
    half = weight_ref.shape[0] // 2
    inside = tile_inside(lengths_ref, row_len, block_len)
    for j in range(block_len):
        projected = lax.dot_general(
            weight_ref[...], norm_ref[j], (((1,), (1,)), ((), ())), preferred_element_type=jnp.float32
        )
        sig = jax.nn.sigmoid(projected[half:])
        kept = sig * inside[j]
        factor_ref[j, :half] = kept.astype(jnp.bfloat16)
        factor_ref[j, half:] = (projected[:half] * kept * (1.0 - sig)).astype(jnp.bfloat16)


def gate_factors(lengths, z_norm, weight_rows, block_len=16):
    col_len, row_len, width = z_norm.shape
    return pl.pallas_call(
        factors_kernel,
        grid=(col_len // block_len,),
        in_specs=[
            pl.BlockSpec(memory_space=pltpu.SMEM),
            pl.BlockSpec((block_len, row_len, width), lambda j: (j, 0, 0)),
            pl.BlockSpec(weight_rows.shape, lambda j: (0, 0)),
        ],
        out_specs=pl.BlockSpec((block_len, weight_rows.shape[0], row_len), lambda j: (j, 0, 0)),
        out_shape=jax.ShapeDtypeStruct((col_len, weight_rows.shape[0], row_len), jnp.bfloat16),
        name="gate_factors",
    )(lengths, z_norm, weight_rows)


def projection_grads(grad_ref, factor_ref):
    hidden_width, _, block_len, row_len = grad_ref.shape
    grads = grad_ref[...].astype(jnp.float32).reshape(2 * hidden_width, block_len, row_len)
    grads = jnp.swapaxes(grads, 0, 1)
    return [
        jnp.concatenate(
            [
                (grads[j] * factor_ref[j, : 2 * hidden_width].astype(jnp.float32)),
                (grads[j] * factor_ref[j, 2 * hidden_width :].astype(jnp.float32)),
            ],
            0,
        ).astype(jnp.bfloat16)
        for j in range(block_len)
    ]


def weight_sums_kernel(grad_ref, factor_ref, norm_ref, gate_ref, out_ref, sum_ref, total_ref):
    hidden_width, _, block_len, row_len = grad_ref.shape
    width = norm_ref.shape[2]
    step = pl.program_id(0)
    grads = jnp.concatenate(projection_grads(grad_ref, factor_ref), 1)
    partial = jnp.dot(
        grads,
        norm_ref[...].reshape(block_len * row_len, width),
        preferred_element_type=jnp.float32,
    )

    @pl.when(step == 0)
    def _():
        total_ref[...] = partial

    @pl.when(step > 0)
    def _():
        total_ref[...] += partial

    @pl.when(step == pl.num_programs(0) - 1)
    def _():
        for side in range(2):
            for kind in range(2):
                rows = total_ref[
                    pl.ds(kind * 2 * hidden_width + side, hidden_width, stride=2), :
                ]
                at = (2 * side + kind) * width
                sum_ref[at : at + width] = rows.T
        sum_ref[4 * width : 5 * width] = gate_ref[...]
        sum_ref[5 * width : 6 * width] = out_ref[...]
        sum_ref[6 * width :] = jnp.zeros((2 * width, width), jnp.float32)


def weight_sums(grad_tiles, factors, z_norm, grad_w_gate, grad_w_out, block_len=16):
    hidden_width, _, col_len, row_len = grad_tiles.shape
    width = z_norm.shape[2]
    square = pl.BlockSpec((width, width), lambda j: (0, 0))
    return pl.pallas_call(
        weight_sums_kernel,
        grid=(col_len // block_len,),
        in_specs=[
            pl.BlockSpec((hidden_width, 2, block_len, row_len), lambda j: (0, 0, j, 0)),
            pl.BlockSpec((block_len, 4 * hidden_width, row_len), lambda j: (j, 0, 0)),
            pl.BlockSpec((block_len, row_len, width), lambda j: (j, 0, 0)),
            square,
            square,
        ],
        out_specs=pl.BlockSpec((8 * width, width), lambda j: (0, 0)),
        out_shape=jax.ShapeDtypeStruct((8 * width, width), jnp.float32),
        scratch_shapes=[pltpu.VMEM((4 * hidden_width, width), jnp.float32)],
        name="weight_sums",
    )(grad_tiles, factors, z_norm, grad_w_gate, grad_w_out)


def pair_grad_kernel(
    pair_ref, grad_ref, factor_ref, gate_ref, weight_ref, w_gate_ref, gain_ref, _, out_ref
):
    block_len = pair_ref.shape[1]
    z_hat, z_inverse = layer_norm(jnp.swapaxes(pair_ref[...].astype(jnp.float32), 0, 1))
    grads = projection_grads(grad_ref, factor_ref)
    grad_norm = []
    for j in range(block_len):
        total = jnp.dot(weight_ref[...], grads[j], preferred_element_type=jnp.float32)
        total += lax.dot_general(
            w_gate_ref[...], gate_ref[j], (((1,), (1,)), ((), ())), preferred_element_type=jnp.float32
        )
        grad_norm.append(total.T)
    grad_hat = jnp.stack(grad_norm, 0) * gain_ref[...]
    grad_pair = normalize_back(grad_hat, z_hat, z_inverse, -1)
    out_ref[...] = jnp.swapaxes(grad_pair, 0, 1).astype(jnp.bfloat16)


def pair_grad(half, into, pair_rep, grad_tiles, factors, grad_gate, w_tri, w_gate, gain, block_len=16):
    row_len, col_len, width = pair_rep.shape
    hidden_width = grad_tiles.shape[0]
    steps = col_len // block_len // 2
    first = half * steps
    return pl.pallas_call(
        pair_grad_kernel,
        grid=(steps,),
        in_specs=[
            pl.BlockSpec((row_len, block_len, width), lambda j: (0, first + j, 0)),
            pl.BlockSpec((hidden_width, 2, block_len, row_len), lambda j: (0, 0, first + j, 0)),
            pl.BlockSpec((block_len, 4 * hidden_width, row_len), lambda j: (first + j, 0, 0)),
            pl.BlockSpec((block_len, row_len, width), lambda j: (first + j, 0, 0)),
            pl.BlockSpec(w_tri.shape, lambda j: (0, 0)),
            pl.BlockSpec(w_gate.shape, lambda j: (0, 0)),
            pl.BlockSpec((1, width), lambda j: (0, 0)),
            pl.BlockSpec(memory_space=pl.ANY),
        ],
        out_specs=pl.BlockSpec((row_len, block_len, width), lambda j: (0, first + j, 0)),
        out_shape=jax.ShapeDtypeStruct(pair_rep.shape, jnp.bfloat16),
        input_output_aliases={7: 0},
        name="pair_grad",
    )(pair_rep, grad_tiles, factors, grad_gate, w_tri, w_gate, gain[None], into)


def finish_kernel(total_ref, w_in_ref, w_out_ref, g_in_ref, g_out_ref, gw_in_ref, gw_out_ref, gg_in_ref, gg_out_ref):
    width = gw_out_ref.shape[0]
    blocks = gw_in_ref.shape[1] // width
    along_in = jnp.zeros((width, 1), jnp.float32)
    for block in range(blocks):
        part = total_ref[block * width : (block + 1) * width] / N
        at = slice(block * width, (block + 1) * width)
        gw_in_ref[:, at] = part
        along_in += jnp.sum(part * w_in_ref[:, at].astype(jnp.float32), axis=1, keepdims=True)
    part = total_ref[blocks * width : (blocks + 1) * width] / N
    gw_out_ref[...] = part
    along_out = jnp.sum(part * w_out_ref[...].astype(jnp.float32), axis=1, keepdims=True)
    gg_in_ref[...] = jnp.broadcast_to(along_in, (width, width)).T[:1] / g_in_ref[...]
    gg_out_ref[...] = jnp.broadcast_to(along_out, (width, width)).T[:1] / g_out_ref[...]


def finish(totals, weight_in, weight_out, gain_in, gain_out):
    row = jax.ShapeDtypeStruct((1, gain_in.shape[0]), jnp.float32)
    grads = pl.pallas_call(
        finish_kernel,
        out_shape=[
            jax.ShapeDtypeStruct(weight_in.shape, jnp.float32),
            jax.ShapeDtypeStruct(weight_out.shape, jnp.float32),
            row,
            row,
        ],
        name="finish",
    )(totals, weight_in, weight_out, gain_in[None], gain_out[None])
    return grads[0], grads[1], grads[2][0], grads[3][0]


def outer_grad_kernel(outer_ref, back_ref, mean_ref, grad_ref):
    o_hat, o_inverse = normalize(outer_ref[...].astype(jnp.float32), 0)
    back = back_ref[...]
    second_mean = jnp.mean(back * o_hat, axis=0, keepdims=True)
    grad = o_inverse * (back - mean_ref[...][None] - o_hat * second_mean)
    grad_ref[...] = grad.astype(jnp.bfloat16)


def outer_grad(outer_tile, back, back_mean, block_len=16):
    hidden_width, col_len, row_len = outer_tile.shape
    whole = pl.BlockSpec((hidden_width, block_len, row_len), lambda j: (0, j, 0))
    return pl.pallas_call(
        outer_grad_kernel,
        grid=(col_len // block_len,),
        in_specs=[whole, whole, pl.BlockSpec((block_len, row_len), lambda j: (j, 0))],
        out_specs=whole,
        out_shape=jax.ShapeDtypeStruct(outer_tile.shape, jnp.bfloat16),
        name="outer_grad",
    )(outer_tile, back, back_mean)


def on_device(pair_rep, cotangent, lengths, weight_in, weight_out, gain_in, gain_out):
    groups = lax.axis_size("grp")
    rows_n = lax.axis_size("row")
    cols_n = lax.axis_size("col")
    devices = rows_n * cols_n
    row_len = pair_rep.shape[1]
    col_len = pair_rep.shape[2]
    width = pair_rep.shape[3]
    hidden_width = weight_out.shape[0]
    share = hidden_width // devices
    lookup = jnp.arange(groups) == lax.axis_index("grp")
    own_length = jnp.sum(jnp.where(lookup, lengths, 0))
    row_in = lax.axis_index("row") * row_len + jnp.arange(row_len) < own_length
    col_in = lax.axis_index("col") * col_len + jnp.arange(col_len) < own_length
    flipped_c = (col_in[:, None] & row_in[None, :]).astype(jnp.float32)[:, :, None]
    w_gate = weight_in[:, 4 * hidden_width :]

    pair_tiles, z_norm = project(lengths, pair_rep[0], weight_in, gain_in)
    pair_ch = exchange(pair_tiles).reshape(devices, share, 2, col_len, row_len)

    w_tri = weight_in[:, : 4 * hidden_width].reshape(width, 2, 2, hidden_width)
    w_tri = w_tri.transpose(0, 2, 3, 1).reshape(width, 4 * hidden_width)
    factors = gate_factors(lengths, z_norm, w_tri.T)
    gate_pre = jnp.einsum("jic,cd->jid", z_norm, w_gate, preferred_element_type=jnp.float32)
    gate = jax.nn.sigmoid(gate_pre) * flipped_c
    grad_out = jnp.swapaxes(cotangent[0], 0, 1).astype(jnp.float32)
    grad_proj = (grad_out * gate).astype(jnp.bfloat16)
    grad_o_norm = jnp.einsum(
        "jic,hc->hji", grad_proj, weight_out, preferred_element_type=jnp.float32
    )
    back = grad_o_norm * gain_out[:, None, None]
    back_mean = jnp.mean(back, axis=0)
    pair_ch, factors, gate, grad_proj, back, back_mean = lax.optimization_barrier(
        (pair_ch, factors, gate, grad_proj, back, back_mean)
    )

    outer_ch = triangle(pair_ch, rows_n, cols_n)
    outer_tile = exchange(outer_ch.reshape(hidden_width, col_len, row_len))
    grad_outer = outer_grad(outer_tile, back, back_mean)
    grad_ch = exchange(grad_outer).reshape(devices, share, col_len, row_len)

    o_hat, _ = normalize(outer_tile.astype(jnp.float32), 0)
    o_norm = (o_hat * gain_out[:, None, None]).astype(jnp.bfloat16)
    proj_out = jnp.einsum("hji,hc->jic", o_norm, weight_out, preferred_element_type=jnp.float32)
    mixed = jnp.swapaxes((gate * proj_out).astype(jnp.bfloat16), 0, 1)
    grad_gate = (grad_out * proj_out * gate * (1.0 - gate)).astype(jnp.bfloat16)
    grad_w_out = jnp.einsum("hji,jic->hc", o_norm, grad_proj, preferred_element_type=jnp.float32)
    grad_w_gate = jnp.einsum("jic,jid->cd", z_norm, grad_gate, preferred_element_type=jnp.float32)

    grad_ch, mixed, grad_gate, grad_w_gate, grad_w_out = lax.optimization_barrier(
        (grad_ch, mixed, grad_gate, grad_w_gate, grad_w_out)
    )
    grad_parts = triangle_back(pair_ch, grad_ch, rows_n, cols_n)
    grad_tiles = exchange(grad_parts.reshape(hidden_width, 2, col_len, row_len))
    sums = weight_sums(grad_tiles, factors, z_norm, grad_w_gate, grad_w_out)
    pieces = sums.reshape(lax.axis_size(ALL), -1, width)
    arrived = lax.all_to_all(pieces, ALL, split_axis=0, concat_axis=0, tiled=True)
    pair_parts = (pair_rep[0], grad_tiles, factors, grad_gate, w_tri, w_gate, gain_in)
    grad_pair = pair_grad(0, z_norm.reshape(pair_rep.shape[1:]), *pair_parts)
    arrived, grad_pair = lax.optimization_barrier((arrived, grad_pair))
    spread = jnp.broadcast_to(jnp.sum(arrived, axis=0, keepdims=True), pieces.shape)
    totals = lax.all_to_all(spread, ALL, split_axis=0, concat_axis=0, tiled=True)
    grad_pair = pair_grad(1, grad_pair, *pair_parts)
    grad_w_in, grad_w_out, grad_g_in, grad_g_out = finish(
        totals.reshape(sums.shape), weight_in, weight_out, gain_in, gain_out
    )
    return (mixed[None], grad_pair[None], grad_w_in, grad_w_out, grad_g_in, grad_g_out)


def solution(mesh):
    return jax.shard_map(
        on_device,
        mesh=mesh,
        in_specs=(
            P("grp", "row", "col", None),
            P("grp", "row", "col", None),
            P(),
            P(),
            P(),
            P(),
            P(),
        ),
        out_specs=(P("grp", "row", "col", None), P("grp", "row", "col", None), P(), P(), P(), P()),
        check_vma=False,
    )
```

```python
import functools

import jax
import jax.numpy as jnp
from jax import lax
from jax.experimental import pallas as pl
from jax.experimental.pallas import tpu as pltpu
from jax.sharding import PartitionSpec as P

N = 512
ALL = ("grp", "row", "col")
TILE = ("row", "col")
STAGGER_NS = 2000


epsilon = 1e-05


def normalize(values, along):
    centred = values - jnp.mean(values, axis=along, keepdims=True)
    inverse = lax.rsqrt(jnp.mean(centred * centred, axis=along, keepdims=True) + epsilon)
    return (centred * inverse, inverse)


def normalize_back(grad_hat, normed, inverse, along):
    first_mean = jnp.mean(grad_hat, axis=along, keepdims=True)
    second_mean = jnp.mean(grad_hat * normed, axis=along, keepdims=True)
    return inverse * (grad_hat - first_mean - normed * second_mean)


def exchange(tiles):
    return lax.all_to_all(tiles, TILE, split_axis=0, concat_axis=0, tiled=True)


def forward_kernel(rows_n, cols_n, pair_ref, out_ref, left_ref, right_ref):
    col_len, row_len = pair_ref.shape[3], pair_ref.shape[4]
    for r in range(rows_n):
        for c in range(cols_n):
            at = (pl.ds(c * col_len, col_len), pl.ds(r * row_len, row_len))
            left_ref[at] = pair_ref[r * cols_n + c, 0, 0]
            right_ref[at] = pair_ref[r * cols_n + c, 0, 1]
    outer = lax.dot_general(
        right_ref[...], left_ref[...], (((0,), (0,)), ((), ())), preferred_element_type=jnp.float32
    ).astype(jnp.bfloat16)
    for r in range(rows_n):
        for c in range(cols_n):
            out_ref[r * cols_n + c, 0] = outer[
                c * col_len : (c + 1) * col_len, r * row_len : (r + 1) * row_len
            ]


def backward_kernel(rows_n, cols_n, pair_ref, grad_ref, out_ref, left_ref, right_ref, outer_ref):
    col_len, row_len = pair_ref.shape[3], pair_ref.shape[4]
    for r in range(rows_n):
        for c in range(cols_n):
            at = (pl.ds(c * col_len, col_len), pl.ds(r * row_len, row_len))
            left_ref[at] = pair_ref[r * cols_n + c, 0, 0]
            right_ref[at] = pair_ref[r * cols_n + c, 0, 1]
            outer_ref[at] = grad_ref[r * cols_n + c, 0]
    grad_left = lax.dot_general(
        right_ref[...], outer_ref[...], (((1,), (0,)), ((), ())), preferred_element_type=jnp.float32
    ).astype(jnp.bfloat16)
    grad_right = lax.dot_general(
        left_ref[...], outer_ref[...], (((1,), (1,)), ((), ())), preferred_element_type=jnp.float32
    ).astype(jnp.bfloat16)
    for r in range(rows_n):
        for c in range(cols_n):
            at = (slice(c * col_len, (c + 1) * col_len), slice(r * row_len, (r + 1) * row_len))
            out_ref[r * cols_n + c, 0, 0] = grad_left[at]
            out_ref[r * cols_n + c, 0, 1] = grad_right[at]


def triangle(pair_ch, rows_n, cols_n):
    devices, share, _, col_len, row_len = pair_ch.shape
    side = cols_n * col_len
    return pl.pallas_call(
        functools.partial(forward_kernel, rows_n, cols_n),
        grid=(share,),
        in_specs=[pl.BlockSpec((devices, 1, 2, col_len, row_len), lambda h: (0, h, 0, 0, 0))],
        out_specs=pl.BlockSpec((devices, 1, col_len, row_len), lambda h: (0, h, 0, 0)),
        out_shape=jax.ShapeDtypeStruct((devices, share, col_len, row_len), jnp.bfloat16),
        scratch_shapes=[pltpu.VMEM((side, side), jnp.bfloat16)] * 2,
        name="triangle_forward",
    )(pair_ch)


def triangle_back(pair_ch, grad_ch, rows_n, cols_n):
    devices, share, _, col_len, row_len = pair_ch.shape
    side = cols_n * col_len
    return pl.pallas_call(
        functools.partial(backward_kernel, rows_n, cols_n),
        grid=(share,),
        in_specs=[
            pl.BlockSpec((devices, 1, 2, col_len, row_len), lambda h: (0, h, 0, 0, 0)),
            pl.BlockSpec((devices, 1, col_len, row_len), lambda h: (0, h, 0, 0)),
        ],
        out_specs=pl.BlockSpec((devices, 1, 2, col_len, row_len), lambda h: (0, h, 0, 0, 0)),
        out_shape=jax.ShapeDtypeStruct(pair_ch.shape, jnp.bfloat16),
        scratch_shapes=[pltpu.VMEM((side, side), jnp.bfloat16)] * 3,
        name="triangle_backward",
    )(pair_ch, grad_ch)


def layer_norm(values):
    centred = values - jnp.mean(values, axis=-1, keepdims=True)
    inverse = lax.rsqrt(jnp.mean(centred * centred, axis=-1, keepdims=True) + epsilon)
    return centred * inverse, inverse


def tile_inside(lengths_ref, row_len, block_len):
    length = lengths_ref[lax.axis_index("grp")]
    row_start = lax.axis_index("row") * row_len
    col_start = (lax.axis_index("col") * pl.num_programs(0) + pl.program_id(0)) * block_len
    row_in = row_start + lax.broadcasted_iota(jnp.int32, (1, row_len), 1) < length
    return [
        jnp.where(row_in & (col_start + j < length), 1.0, 0.0).astype(jnp.float32)
        for j in range(block_len)
    ]


def project_kernel(lengths_ref, pair_ref, weight_ref, gain_ref, tile_ref, norm_ref, rows_ref):
    row_len, block_len, _ = pair_ref.shape
    hidden_width = tile_ref.shape[0]
    first = pl.program_id(0) == 0

    @pl.when(first)
    def _():
        for at, source in enumerate((0, 2, 1, 3)):
            part = weight_ref[:, source * hidden_width : (source + 1) * hidden_width]
            rows_ref[at * hidden_width : (at + 1) * hidden_width] = part.astype(jnp.float32).T.astype(
                jnp.bfloat16
            )

    normed, _ = layer_norm(jnp.swapaxes(pair_ref[...].astype(jnp.float32), 0, 1))
    normed = (normed * gain_ref[...]).astype(jnp.bfloat16)
    norm_ref[...] = normed
    inside = tile_inside(lengths_ref, row_len, block_len)
    gated = []
    for j in range(block_len):
        projected = lax.dot_general(
            rows_ref[...], normed[j], (((1,), (1,)), ((), ())), preferred_element_type=jnp.float32
        )
        sig = jax.nn.sigmoid(projected[2 * hidden_width :])
        gated.append(projected[: 2 * hidden_width] * sig * inside[j])
    gated = jnp.swapaxes(jnp.stack(gated, 0), 0, 1).astype(jnp.bfloat16)
    tile_ref[:, 0] = gated[:hidden_width]
    tile_ref[:, 1] = gated[hidden_width:]


def project(lengths, pair_rep, weight_in, gain, block_len=16):
    row_len, col_len, width = pair_rep.shape
    hidden_width = (weight_in.shape[1] - width) // 4
    return pl.pallas_call(
        project_kernel,
        grid=(col_len // block_len,),
        in_specs=[
            pl.BlockSpec(memory_space=pltpu.SMEM),
            pl.BlockSpec((row_len, block_len, width), lambda j: (0, j, 0)),
            pl.BlockSpec(weight_in.shape, lambda j: (0, 0)),
            pl.BlockSpec((1, width), lambda j: (0, 0)),
        ],
        out_specs=[
            pl.BlockSpec((hidden_width, 2, block_len, row_len), lambda j: (0, 0, j, 0)),
            pl.BlockSpec((block_len, row_len, width), lambda j: (j, 0, 0)),
        ],
        out_shape=[
            jax.ShapeDtypeStruct((hidden_width, 2, col_len, row_len), jnp.bfloat16),
            jax.ShapeDtypeStruct((col_len, row_len, width), jnp.bfloat16),
        ],
        scratch_shapes=[pltpu.VMEM((4 * hidden_width, width), jnp.bfloat16)],
        name="project",
    )(lengths, pair_rep, weight_in, gain[None])


def side_kernel(
    lengths_ref,
    weight_ref,
    w_gate_ref,
    w_out_ref,
    gain_ref,
    norm_ref,
    cotangent_ref,
    factor_ref,
    gate_ref,
    grad_proj_ref,
    back_ref,
    mean_ref,
):
    block_len, row_len, width = norm_ref.shape
    half = weight_ref.shape[0] // 2
    inside = tile_inside(lengths_ref, row_len, block_len)
    grad_out = jnp.swapaxes(cotangent_ref[...].astype(jnp.float32), 0, 1)
    length = lengths_ref[lax.axis_index("grp")]
    row_at = lax.axis_index("row") * row_len + lax.broadcasted_iota(jnp.int32, (row_len, 1), 0)
    col_start = (lax.axis_index("col") * pl.num_programs(0) + pl.program_id(0)) * block_len
    backs = []
    for j in range(block_len):
        projected = lax.dot_general(
            weight_ref[...], norm_ref[j], (((1,), (1,)), ((), ())), preferred_element_type=jnp.float32
        )
        sig = jax.nn.sigmoid(projected[half:])
        kept = sig * inside[j]
        factor_ref[j, :half] = kept.astype(jnp.bfloat16)
        factor_ref[j, half:] = (projected[:half] * kept * (1.0 - sig)).astype(jnp.bfloat16)
        here = jnp.where((row_at < length) & (col_start + j < length), 1.0, 0.0)
        gate_pre = jnp.dot(norm_ref[j], w_gate_ref[...], preferred_element_type=jnp.float32)
        gate = jax.nn.sigmoid(gate_pre) * here
        gate_ref[j] = gate
        grad_proj = (grad_out[j] * gate).astype(jnp.bfloat16)
        grad_proj_ref[j] = grad_proj
        back = gain_ref[...] * lax.dot_general(
            w_out_ref[...], grad_proj, (((1,), (1,)), ((), ())), preferred_element_type=jnp.float32
        )
        mean_ref[j : j + 1] = jnp.mean(back, axis=0, keepdims=True)
        backs.append(back)
    back_ref[...] = jnp.swapaxes(jnp.stack(backs, 0), 0, 1)


def gain_rows(gain_ref):
    width = gain_ref.shape[1]
    return jnp.broadcast_to(gain_ref[...], (width, width)).T


def side_pipeline(odd, specs_in, specs_out, steps, lengths_ref, weight_ref, w_out_ref, gain_ref, *refs):
    *refs, wide_ref, rows_ref, spread_ref = refs
    inputs, outputs = refs[: len(specs_in)], refs[-len(specs_out) :]
    width = w_out_ref.shape[0]

    @pl.when(lax.axis_index("grp") % 2 == odd)
    def _():
        if odd and STAGGER_NS:
            pl.delay(STAGGER_NS)
        for side in range(2):
            for kind in range(2):
                source = (2 * side + kind) * width
                part = weight_ref[:, source : source + width].astype(jnp.float32).T
                wide_ref[pl.ds(kind * 2 * width + side, width, stride=2), :] = part
        rows_ref[...] = wide_ref[...].astype(jnp.bfloat16)
        spread_ref[...] = gain_rows(gain_ref)
        w_gate_ref = weight_ref.at[:, 4 * width :]
        pltpu.emit_pipeline(
            functools.partial(side_kernel, lengths_ref, rows_ref, w_gate_ref, w_out_ref, spread_ref),
            grid=(steps,),
            in_specs=specs_in,
            out_specs=specs_out,
        )(*inputs, *outputs)


def side_work(odd, into, lengths, weight_in, w_out, gain_out, z_norm, cotangent, block_len=16):
    col_len, row_len, width = z_norm.shape
    hidden_width = w_out.shape[0]
    by_pair = pl.BlockSpec((block_len, row_len, width), lambda j: (j, 0, 0))
    specs_in = [by_pair, pl.BlockSpec((row_len, block_len, width), lambda j: (0, j, 0))]
    specs_out = [
        pl.BlockSpec((block_len, 4 * hidden_width, row_len), lambda j: (j, 0, 0)),
        by_pair,
        by_pair,
        pl.BlockSpec((hidden_width, block_len, row_len), lambda j: (0, j, 0)),
        pl.BlockSpec((block_len, row_len), lambda j: (j, 0)),
    ]
    anywhere = pl.BlockSpec(memory_space=pl.ANY)
    in_vmem = pl.BlockSpec(memory_space=pltpu.VMEM)
    return pl.pallas_call(
        functools.partial(side_pipeline, odd, specs_in, specs_out, col_len // block_len),
        in_specs=[pl.BlockSpec(memory_space=pltpu.SMEM)] + [in_vmem] * 3 + [anywhere] * (2 + len(into)),
        out_specs=[anywhere] * len(specs_out),
        out_shape=[
            pltpu.HBM((col_len, 4 * hidden_width, row_len), jnp.bfloat16),
            pltpu.HBM(z_norm.shape, jnp.float32),
            pltpu.HBM(z_norm.shape, jnp.bfloat16),
            pltpu.HBM((hidden_width, col_len, row_len), jnp.float32),
            pltpu.HBM((col_len, row_len), jnp.float32),
        ],
        scratch_shapes=[
            pltpu.VMEM((4 * hidden_width, width), jnp.float32),
            pltpu.VMEM((4 * hidden_width, width), jnp.bfloat16),
            pltpu.VMEM((hidden_width, width), jnp.float32),
        ],
        input_output_aliases={6 + at: at for at in range(len(into))},
        name="side_work",
    )(lengths, weight_in, w_out, gain_out[None], z_norm, cotangent, *into)


def projection_grads(grad_ref, factor_ref):
    hidden_width, _, block_len, row_len = grad_ref.shape
    grads = grad_ref[...].astype(jnp.float32).reshape(2 * hidden_width, block_len, row_len)
    grads = jnp.swapaxes(grads, 0, 1)
    return [
        jnp.concatenate(
            [
                (grads[j] * factor_ref[j, : 2 * hidden_width].astype(jnp.float32)),
                (grads[j] * factor_ref[j, 2 * hidden_width :].astype(jnp.float32)),
            ],
            0,
        ).astype(jnp.bfloat16)
        for j in range(block_len)
    ]


def block_output_kernel(
    outer_ref, gate_ref, grad_proj_ref, cotangent_ref, norm_ref, w_out_ref, gain_ref,
    mixed_ref, grad_gate_ref, sum_out_ref, sum_gate_ref,
):
    hidden_width, block_len, row_len = outer_ref.shape
    width = norm_ref.shape[2]
    o_hat, _ = normalize(outer_ref[...].astype(jnp.float32), 0)
    o_hat = jnp.swapaxes(o_hat, 0, 1)
    grad_out = jnp.swapaxes(cotangent_ref[...].astype(jnp.float32), 0, 1)
    spread = gain_rows(gain_ref)
    normed, mixed = [], []
    for j in range(block_len):
        o_norm = (o_hat[j] * spread).astype(jnp.bfloat16)
        normed.append(o_norm)
        proj_out = lax.dot_general(
            o_norm, w_out_ref[...], (((0,), (0,)), ((), ())), preferred_element_type=jnp.float32
        )
        gate = gate_ref[j]
        mixed.append(gate * proj_out)
        grad_gate_ref[j] = (grad_out[j] * proj_out * gate * (1.0 - gate)).astype(jnp.bfloat16)
    mixed_ref[...] = jnp.swapaxes(jnp.stack(mixed, 0), 0, 1).astype(jnp.bfloat16)
    flat = (block_len * row_len, width)
    sum_out = jnp.dot(
        jnp.concatenate(normed, 1), grad_proj_ref[...].reshape(flat), preferred_element_type=jnp.float32
    )
    sum_gate = lax.dot_general(
        norm_ref[...].reshape(flat),
        grad_gate_ref[...].reshape(flat),
        (((0,), (0,)), ((), ())),
        preferred_element_type=jnp.float32,
    )

    @pl.when(pl.program_id(0) == 0)
    def _():
        sum_out_ref[...] = sum_out
        sum_gate_ref[...] = sum_gate

    @pl.when(pl.program_id(0) > 0)
    def _():
        sum_out_ref[...] += sum_out
        sum_gate_ref[...] += sum_gate


def block_output(outer_tile, gate, grad_proj, cotangent, z_norm, w_out, gain_out, block_len=16):
    hidden_width, col_len, row_len = outer_tile.shape
    width = z_norm.shape[2]
    by_pair = pl.BlockSpec((block_len, row_len, width), lambda j: (j, 0, 0))
    natural = pl.BlockSpec((row_len, block_len, width), lambda j: (0, j, 0))
    square = pl.BlockSpec((width, width), lambda j: (0, 0))
    return pl.pallas_call(
        block_output_kernel,
        grid=(col_len // block_len,),
        in_specs=[
            pl.BlockSpec((hidden_width, block_len, row_len), lambda j: (0, j, 0)),
            by_pair,
            by_pair,
            natural,
            by_pair,
            square,
            pl.BlockSpec((1, width), lambda j: (0, 0)),
        ],
        out_specs=[natural, by_pair, square, square],
        out_shape=[
            pltpu.HBM(cotangent.shape, jnp.bfloat16),
            jax.ShapeDtypeStruct(z_norm.shape, jnp.bfloat16),
            jax.ShapeDtypeStruct((width, width), jnp.float32),
            jax.ShapeDtypeStruct((width, width), jnp.float32),
        ],
        name="block_output",
    )(outer_tile, gate, grad_proj, cotangent, z_norm, w_out, gain_out[None])


def weight_sums_kernel(grad_ref, factor_ref, norm_ref, gate_ref, out_ref, sum_ref, total_ref):
    hidden_width, _, block_len, row_len = grad_ref.shape
    width = norm_ref.shape[2]
    step = pl.program_id(0)
    grads = jnp.concatenate(projection_grads(grad_ref, factor_ref), 1)
    partial = jnp.dot(
        grads,
        norm_ref[...].reshape(block_len * row_len, width),
        preferred_element_type=jnp.float32,
    )

    @pl.when(step == 0)
    def _():
        total_ref[...] = partial

    @pl.when(step > 0)
    def _():
        total_ref[...] += partial

    @pl.when(step == pl.num_programs(0) - 1)
    def _():
        for side in range(2):
            for kind in range(2):
                rows = total_ref[
                    pl.ds(kind * 2 * hidden_width + side, hidden_width, stride=2), :
                ]
                at = (2 * side + kind) * width
                sum_ref[at : at + width] = rows.T
        sum_ref[4 * width : 5 * width] = gate_ref[...]
        sum_ref[5 * width : 6 * width] = out_ref[...]
        sum_ref[6 * width :] = jnp.zeros((2 * width, width), jnp.float32)


def weight_sums(grad_tiles, factors, z_norm, grad_w_gate, grad_w_out, block_len=16):
    hidden_width, _, col_len, row_len = grad_tiles.shape
    width = z_norm.shape[2]
    square = pl.BlockSpec((width, width), lambda j: (0, 0))
    return pl.pallas_call(
        weight_sums_kernel,
        grid=(col_len // block_len,),
        in_specs=[
            pl.BlockSpec((hidden_width, 2, block_len, row_len), lambda j: (0, 0, j, 0)),
            pl.BlockSpec((block_len, 4 * hidden_width, row_len), lambda j: (j, 0, 0)),
            pl.BlockSpec((block_len, row_len, width), lambda j: (j, 0, 0)),
            square,
            square,
        ],
        out_specs=pl.BlockSpec((8 * width, width), lambda j: (0, 0)),
        out_shape=jax.ShapeDtypeStruct((8 * width, width), jnp.float32),
        scratch_shapes=[pltpu.VMEM((4 * hidden_width, width), jnp.float32)],
        name="weight_sums",
    )(grad_tiles, factors, z_norm, grad_w_gate, grad_w_out)


def pair_grad_kernel(
    pair_ref, grad_ref, factor_ref, gate_ref, weight_ref, w_gate_ref, gain_ref, _, out_ref
):
    block_len = pair_ref.shape[1]
    z_hat, z_inverse = layer_norm(jnp.swapaxes(pair_ref[...].astype(jnp.float32), 0, 1))
    grads = projection_grads(grad_ref, factor_ref)
    grad_norm = []
    for j in range(block_len):
        total = jnp.dot(weight_ref[...], grads[j], preferred_element_type=jnp.float32)
        total += lax.dot_general(
            w_gate_ref[...], gate_ref[j], (((1,), (1,)), ((), ())), preferred_element_type=jnp.float32
        )
        grad_norm.append(total.T)
    grad_hat = jnp.stack(grad_norm, 0) * gain_ref[...]
    grad_pair = normalize_back(grad_hat, z_hat, z_inverse, -1)
    out_ref[...] = jnp.swapaxes(grad_pair, 0, 1).astype(jnp.bfloat16)


def pair_grad(half, into, pair_rep, grad_tiles, factors, grad_gate, w_tri, w_gate, gain, block_len=16):
    row_len, col_len, width = pair_rep.shape
    hidden_width = grad_tiles.shape[0]
    steps = col_len // block_len // 2
    first = half * steps
    return pl.pallas_call(
        pair_grad_kernel,
        grid=(steps,),
        in_specs=[
            pl.BlockSpec((row_len, block_len, width), lambda j: (0, first + j, 0)),
            pl.BlockSpec((hidden_width, 2, block_len, row_len), lambda j: (0, 0, first + j, 0)),
            pl.BlockSpec((block_len, 4 * hidden_width, row_len), lambda j: (first + j, 0, 0)),
            pl.BlockSpec((block_len, row_len, width), lambda j: (first + j, 0, 0)),
            pl.BlockSpec(w_tri.shape, lambda j: (0, 0)),
            pl.BlockSpec(w_gate.shape, lambda j: (0, 0)),
            pl.BlockSpec((1, width), lambda j: (0, 0)),
            pl.BlockSpec(memory_space=pl.ANY),
        ],
        out_specs=pl.BlockSpec((row_len, block_len, width), lambda j: (0, first + j, 0)),
        out_shape=jax.ShapeDtypeStruct(pair_rep.shape, jnp.bfloat16),
        input_output_aliases={7: 0},
        name="pair_grad",
    )(pair_rep, grad_tiles, factors, grad_gate, w_tri, w_gate, gain[None], into)


def finish_kernel(total_ref, w_in_ref, w_out_ref, g_in_ref, g_out_ref, gw_in_ref, gw_out_ref, gg_in_ref, gg_out_ref):
    width = gw_out_ref.shape[0]
    blocks = gw_in_ref.shape[1] // width
    along_in = jnp.zeros((width, 1), jnp.float32)
    for block in range(blocks):
        part = total_ref[block * width : (block + 1) * width] / N
        at = slice(block * width, (block + 1) * width)
        gw_in_ref[:, at] = part
        along_in += jnp.sum(part * w_in_ref[:, at].astype(jnp.float32), axis=1, keepdims=True)
    part = total_ref[blocks * width : (blocks + 1) * width] / N
    gw_out_ref[...] = part
    along_out = jnp.sum(part * w_out_ref[...].astype(jnp.float32), axis=1, keepdims=True)
    gg_in_ref[...] = jnp.broadcast_to(along_in, (width, width)).T[:1] / g_in_ref[...]
    gg_out_ref[...] = jnp.broadcast_to(along_out, (width, width)).T[:1] / g_out_ref[...]


def finish(totals, weight_in, weight_out, gain_in, gain_out):
    row = jax.ShapeDtypeStruct((1, gain_in.shape[0]), jnp.float32)
    grads = pl.pallas_call(
        finish_kernel,
        out_shape=[
            jax.ShapeDtypeStruct(weight_in.shape, jnp.float32),
            jax.ShapeDtypeStruct(weight_out.shape, jnp.float32),
            row,
            row,
        ],
        name="finish",
    )(totals, weight_in, weight_out, gain_in[None], gain_out[None])
    return grads[0], grads[1], grads[2][0], grads[3][0]


def outer_grad_kernel(outer_ref, back_ref, mean_ref, grad_ref):
    hidden_width = outer_ref.shape[0]
    zero = jnp.zeros(mean_ref.shape, jnp.float32)

    def over_channels(step, start):
        return lax.fori_loop(0, hidden_width, step, start, unroll=16)

    mean = over_channels(lambda h, run: run + outer_ref[h].astype(jnp.float32), zero) / hidden_width

    def products(h, run):
        centred = outer_ref[h].astype(jnp.float32) - mean
        return run[0] + centred * centred, run[1] + centred * back_ref[h]

    square, cross = over_channels(products, (zero, zero))
    inverse = lax.rsqrt(square / hidden_width + epsilon)
    slope = inverse * inverse * inverse * (cross / hidden_width)
    offset = inverse * mean_ref[...]

    def write(h, run):
        centred = outer_ref[h].astype(jnp.float32) - mean
        grad_ref[h] = (inverse * back_ref[h] - offset - centred * slope).astype(jnp.bfloat16)
        return run

    over_channels(write, 0)


def outer_grad(outer_tile, back, back_mean, block_len=16):
    hidden_width, col_len, row_len = outer_tile.shape
    whole = pl.BlockSpec((hidden_width, block_len, row_len), lambda j: (0, j, 0))
    return pl.pallas_call(
        outer_grad_kernel,
        grid=(col_len // block_len,),
        in_specs=[whole, whole, pl.BlockSpec((block_len, row_len), lambda j: (j, 0))],
        out_specs=whole,
        out_shape=jax.ShapeDtypeStruct(outer_tile.shape, jnp.bfloat16),
        name="outer_grad",
    )(outer_tile, back, back_mean)


def on_device(pair_rep, cotangent, lengths, weight_in, weight_out, gain_in, gain_out):
    rows_n = lax.axis_size("row")
    cols_n = lax.axis_size("col")
    devices = rows_n * cols_n
    row_len = pair_rep.shape[1]
    col_len = pair_rep.shape[2]
    width = pair_rep.shape[3]
    hidden_width = weight_out.shape[0]
    share = hidden_width // devices

    pair_tiles, z_norm = project(lengths, pair_rep[0], weight_in, gain_in)
    side_args = (lengths, weight_in, weight_out, gain_out, z_norm, cotangent[0])
    side = side_work(1, (), *side_args)
    pair_tiles, *side = lax.optimization_barrier((pair_tiles, *side))
    pair_ch = exchange(pair_tiles).reshape(devices, share, 2, col_len, row_len)
    outer_ch = triangle(pair_ch, rows_n, cols_n)
    outer_ch, *side = lax.optimization_barrier((outer_ch, *side))
    outer_tile = exchange(outer_ch.reshape(hidden_width, col_len, row_len))
    side = side_work(0, tuple(side), *side_args)
    outer_tile, *side = lax.optimization_barrier((outer_tile, *side))
    factors, gate, grad_proj, back, back_mean = side
    grad_outer = outer_grad(outer_tile, back, back_mean)
    grad_ch = exchange(grad_outer).reshape(devices, share, col_len, row_len)

    mixed, grad_gate, grad_w_out, grad_w_gate = block_output(
        outer_tile, gate, grad_proj, cotangent[0], z_norm, weight_out, gain_out
    )
    grad_ch, mixed, grad_gate, grad_w_gate, grad_w_out = lax.optimization_barrier(
        (grad_ch, mixed, grad_gate, grad_w_gate, grad_w_out)
    )
    grad_parts = triangle_back(pair_ch, grad_ch, rows_n, cols_n)
    grad_tiles = exchange(grad_parts.reshape(hidden_width, 2, col_len, row_len))
    grad_tiles, late_weight = lax.optimization_barrier((grad_tiles, weight_in))
    w_tri = late_weight[:, : 4 * hidden_width].reshape(width, 2, 2, hidden_width)
    w_tri = w_tri.transpose(0, 2, 3, 1).reshape(width, 4 * hidden_width)
    w_gate = late_weight[:, 4 * hidden_width :]
    sums = weight_sums(grad_tiles, factors, z_norm, grad_w_gate, grad_w_out)
    pieces = sums.reshape(lax.axis_size(ALL), -1, width)
    arrived = lax.all_to_all(pieces, ALL, split_axis=0, concat_axis=0, tiled=True)
    pair_parts = (pair_rep[0], grad_tiles, factors, grad_gate, w_tri, w_gate, gain_in)
    grad_pair = pair_grad(0, z_norm.reshape(pair_rep.shape[1:]), *pair_parts)
    arrived, grad_pair = lax.optimization_barrier((arrived, grad_pair))
    spread = jnp.broadcast_to(jnp.sum(arrived, axis=0, keepdims=True), pieces.shape)
    totals = lax.all_to_all(spread, ALL, split_axis=0, concat_axis=0, tiled=True)
    grad_pair = pair_grad(1, grad_pair, *pair_parts)
    grad_w_in, grad_w_out, grad_g_in, grad_g_out = finish(
        totals.reshape(sums.shape), weight_in, weight_out, gain_in, gain_out
    )
    return (mixed[None], grad_pair[None], grad_w_in, grad_w_out, grad_g_in, grad_g_out)


def solution(mesh):
    return jax.shard_map(
        on_device,
        mesh=mesh,
        in_specs=(
            P("grp", "row", "col", None),
            P("grp", "row", "col", None),
            P(),
            P(),
            P(),
            P(),
            P(),
        ),
        out_specs=(P("grp", "row", "col", None), P("grp", "row", "col", None), P(), P(), P(), P()),
        check_vma=False,
    )
```

```python
import functools

import jax
import jax.numpy as jnp
from jax import lax
from jax.experimental import pallas as pl
from jax.experimental.pallas import tpu as pltpu
from jax.sharding import PartitionSpec as P

N = 512
ALL = ("grp", "row", "col")
TILE = ("row", "col")
STAGGER_NS = 7000


epsilon = 1e-05


def normalize(values, along):
    centred = values - jnp.mean(values, axis=along, keepdims=True)
    inverse = lax.rsqrt(jnp.mean(centred * centred, axis=along, keepdims=True) + epsilon)
    return (centred * inverse, inverse)


def normalize_back(grad_hat, normed, inverse, along):
    first_mean = jnp.mean(grad_hat, axis=along, keepdims=True)
    second_mean = jnp.mean(grad_hat * normed, axis=along, keepdims=True)
    return inverse * (grad_hat - first_mean - normed * second_mean)


def exchange(tiles):
    return lax.all_to_all(tiles, TILE, split_axis=0, concat_axis=0, tiled=True)


def forward_kernel(rows_n, cols_n, pair_ref, out_ref, left_ref, right_ref):
    col_len, row_len = pair_ref.shape[3], pair_ref.shape[4]
    for r in range(rows_n):
        for c in range(cols_n):
            at = (pl.ds(c * col_len, col_len), pl.ds(r * row_len, row_len))
            left_ref[at] = pair_ref[r * cols_n + c, 0, 0]
            right_ref[at] = pair_ref[r * cols_n + c, 0, 1]
    outer = lax.dot_general(
        right_ref[...], left_ref[...], (((0,), (0,)), ((), ())), preferred_element_type=jnp.float32
    ).astype(jnp.bfloat16)
    for r in range(rows_n):
        for c in range(cols_n):
            out_ref[r * cols_n + c, 0] = outer[
                c * col_len : (c + 1) * col_len, r * row_len : (r + 1) * row_len
            ]


def backward_kernel(rows_n, cols_n, pair_ref, grad_ref, out_ref, left_ref, right_ref, outer_ref):
    col_len, row_len = pair_ref.shape[3], pair_ref.shape[4]
    for r in range(rows_n):
        for c in range(cols_n):
            at = (pl.ds(c * col_len, col_len), pl.ds(r * row_len, row_len))
            left_ref[at] = pair_ref[r * cols_n + c, 0, 0]
            right_ref[at] = pair_ref[r * cols_n + c, 0, 1]
            outer_ref[at] = grad_ref[r * cols_n + c, 0]
    grad_left = lax.dot_general(
        right_ref[...], outer_ref[...], (((1,), (0,)), ((), ())), preferred_element_type=jnp.float32
    ).astype(jnp.bfloat16)
    grad_right = lax.dot_general(
        left_ref[...], outer_ref[...], (((1,), (1,)), ((), ())), preferred_element_type=jnp.float32
    ).astype(jnp.bfloat16)
    for r in range(rows_n):
        for c in range(cols_n):
            at = (slice(c * col_len, (c + 1) * col_len), slice(r * row_len, (r + 1) * row_len))
            out_ref[r * cols_n + c, 0, 0] = grad_left[at]
            out_ref[r * cols_n + c, 0, 1] = grad_right[at]


def triangle(pair_ch, rows_n, cols_n):
    devices, share, _, col_len, row_len = pair_ch.shape
    side = cols_n * col_len
    return pl.pallas_call(
        functools.partial(forward_kernel, rows_n, cols_n),
        grid=(share,),
        in_specs=[pl.BlockSpec((devices, 1, 2, col_len, row_len), lambda h: (0, h, 0, 0, 0))],
        out_specs=pl.BlockSpec((devices, 1, col_len, row_len), lambda h: (0, h, 0, 0)),
        out_shape=jax.ShapeDtypeStruct((devices, share, col_len, row_len), jnp.bfloat16),
        scratch_shapes=[pltpu.VMEM((side, side), jnp.bfloat16)] * 2,
        name="triangle_forward",
    )(pair_ch)


def triangle_back(pair_ch, grad_ch, rows_n, cols_n):
    devices, share, _, col_len, row_len = pair_ch.shape
    side = cols_n * col_len
    return pl.pallas_call(
        functools.partial(backward_kernel, rows_n, cols_n),
        grid=(share,),
        in_specs=[
            pl.BlockSpec((devices, 1, 2, col_len, row_len), lambda h: (0, h, 0, 0, 0)),
            pl.BlockSpec((devices, 1, col_len, row_len), lambda h: (0, h, 0, 0)),
        ],
        out_specs=pl.BlockSpec((devices, 1, 2, col_len, row_len), lambda h: (0, h, 0, 0, 0)),
        out_shape=pltpu.HBM(pair_ch.shape, jnp.bfloat16),
        scratch_shapes=[pltpu.VMEM((side, side), jnp.bfloat16)] * 3,
        compiler_params=pltpu.CompilerParams(vmem_limit_bytes=48 << 20),
        name="triangle_backward",
    )(pair_ch, grad_ch)


def layer_norm(values):
    centred = values - jnp.mean(values, axis=-1, keepdims=True)
    inverse = lax.rsqrt(jnp.mean(centred * centred, axis=-1, keepdims=True) + epsilon)
    return centred * inverse, inverse


def tile_inside(lengths_ref, row_len, block_len):
    length = lengths_ref[lax.axis_index("grp")]
    row_start = lax.axis_index("row") * row_len
    col_start = (lax.axis_index("col") * pl.num_programs(0) + pl.program_id(0)) * block_len
    row_in = row_start + lax.broadcasted_iota(jnp.int32, (1, row_len), 1) < length
    return [
        jnp.where(row_in & (col_start + j < length), 1.0, 0.0).astype(jnp.float32)
        for j in range(block_len)
    ]


def project_kernel(lengths_ref, pair_ref, weight_ref, gain_ref, tile_ref, norm_ref, rows_ref):
    row_len, block_len, _ = pair_ref.shape
    hidden_width = tile_ref.shape[0]
    first = pl.program_id(0) == 0

    @pl.when(first)
    def _():
        for at, source in enumerate((0, 2, 1, 3)):
            part = weight_ref[:, source * hidden_width : (source + 1) * hidden_width]
            rows_ref[at * hidden_width : (at + 1) * hidden_width] = part.astype(jnp.float32).T.astype(
                jnp.bfloat16
            )

    normed, _ = layer_norm(jnp.swapaxes(pair_ref[...].astype(jnp.float32), 0, 1))
    normed = (normed * gain_ref[...]).astype(jnp.bfloat16)
    norm_ref[...] = normed
    inside = tile_inside(lengths_ref, row_len, block_len)
    gated = []
    for j in range(block_len):
        projected = lax.dot_general(
            rows_ref[...], normed[j], (((1,), (1,)), ((), ())), preferred_element_type=jnp.float32
        )
        sig = jax.nn.sigmoid(projected[2 * hidden_width :])
        gated.append(projected[: 2 * hidden_width] * sig * inside[j])
    gated = jnp.swapaxes(jnp.stack(gated, 0), 0, 1).astype(jnp.bfloat16)
    tile_ref[:, 0] = gated[:hidden_width]
    tile_ref[:, 1] = gated[hidden_width:]


def project(lengths, pair_rep, weight_in, gain, block_len=16):
    row_len, col_len, width = pair_rep.shape
    hidden_width = (weight_in.shape[1] - width) // 4
    return pl.pallas_call(
        project_kernel,
        grid=(col_len // block_len,),
        in_specs=[
            pl.BlockSpec(memory_space=pltpu.SMEM),
            pl.BlockSpec((row_len, block_len, width), lambda j: (0, j, 0)),
            pl.BlockSpec(weight_in.shape, lambda j: (0, 0)),
            pl.BlockSpec((1, width), lambda j: (0, 0)),
        ],
        out_specs=[
            pl.BlockSpec((hidden_width, 2, block_len, row_len), lambda j: (0, 0, j, 0)),
            pl.BlockSpec((block_len, row_len, width), lambda j: (j, 0, 0)),
        ],
        out_shape=[
            jax.ShapeDtypeStruct((hidden_width, 2, col_len, row_len), jnp.bfloat16),
            jax.ShapeDtypeStruct((col_len, row_len, width), jnp.bfloat16),
        ],
        scratch_shapes=[pltpu.VMEM((4 * hidden_width, width), jnp.bfloat16)],
        name="project",
    )(lengths, pair_rep, weight_in, gain[None])


def side_kernel(
    lengths_ref,
    weight_ref,
    w_gate_ref,
    w_out_ref,
    gain_ref,
    norm_ref,
    cotangent_ref,
    factor_ref,
    gate_ref,
    grad_proj_ref,
    back_ref,
    mean_ref,
):
    block_len, row_len, width = norm_ref.shape
    half = weight_ref.shape[0] // 2
    inside = tile_inside(lengths_ref, row_len, block_len)
    grad_out = jnp.swapaxes(cotangent_ref[...].astype(jnp.float32), 0, 1)
    length = lengths_ref[lax.axis_index("grp")]
    row_at = lax.axis_index("row") * row_len + lax.broadcasted_iota(jnp.int32, (row_len, 1), 0)
    col_start = (lax.axis_index("col") * pl.num_programs(0) + pl.program_id(0)) * block_len
    backs = []
    for j in range(block_len):
        projected = lax.dot_general(
            weight_ref[...], norm_ref[j], (((1,), (1,)), ((), ())), preferred_element_type=jnp.float32
        )
        sig = jax.nn.sigmoid(projected[half:])
        kept = sig * inside[j]
        factor_ref[j, :half] = kept.astype(jnp.bfloat16)
        factor_ref[j, half:] = (projected[:half] * kept * (1.0 - sig)).astype(jnp.bfloat16)
        here = jnp.where((row_at < length) & (col_start + j < length), 1.0, 0.0)
        gate_pre = jnp.dot(norm_ref[j], w_gate_ref[...], preferred_element_type=jnp.float32)
        gate = jax.nn.sigmoid(gate_pre) * here
        gate_ref[j] = gate
        grad_proj = (grad_out[j] * gate).astype(jnp.bfloat16)
        grad_proj_ref[j] = grad_proj
        back = gain_ref[...] * lax.dot_general(
            w_out_ref[...], grad_proj, (((1,), (1,)), ((), ())), preferred_element_type=jnp.float32
        )
        mean_ref[j : j + 1] = jnp.mean(back, axis=0, keepdims=True)
        backs.append(back)
    back_ref[...] = jnp.swapaxes(jnp.stack(backs, 0), 0, 1)


def gain_rows(gain_ref):
    width = gain_ref.shape[1]
    return jnp.broadcast_to(gain_ref[...], (width, width)).T


def side_pipeline(odd, specs_in, specs_out, steps, lengths_ref, weight_ref, w_out_ref, gain_ref, *refs):
    *refs, wide_ref, rows_ref, spread_ref = refs
    inputs, outputs = refs[: len(specs_in)], refs[-len(specs_out) :]
    width = w_out_ref.shape[0]

    @pl.when(lax.axis_index("grp") % 2 == odd)
    def _():
        if odd and STAGGER_NS:
            pl.delay(STAGGER_NS)
        for side in range(2):
            for kind in range(2):
                source = (2 * side + kind) * width
                part = weight_ref[:, source : source + width].astype(jnp.float32).T
                wide_ref[pl.ds(kind * 2 * width + side, width, stride=2), :] = part
        rows_ref[...] = wide_ref[...].astype(jnp.bfloat16)
        spread_ref[...] = gain_rows(gain_ref)
        w_gate_ref = weight_ref.at[:, 4 * width :]
        pltpu.emit_pipeline(
            functools.partial(side_kernel, lengths_ref, rows_ref, w_gate_ref, w_out_ref, spread_ref),
            grid=(steps,),
            in_specs=specs_in,
            out_specs=specs_out,
        )(*inputs, *outputs)


def side_work(odd, into, lengths, weight_in, w_out, gain_out, z_norm, cotangent, block_len=16):
    col_len, row_len, width = z_norm.shape
    hidden_width = w_out.shape[0]
    by_pair = pl.BlockSpec((block_len, row_len, width), lambda j: (j, 0, 0))
    specs_in = [by_pair, pl.BlockSpec((row_len, block_len, width), lambda j: (0, j, 0))]
    specs_out = [
        pl.BlockSpec((block_len, 4 * hidden_width, row_len), lambda j: (j, 0, 0)),
        by_pair,
        by_pair,
        pl.BlockSpec((hidden_width, block_len, row_len), lambda j: (0, j, 0)),
        pl.BlockSpec((block_len, row_len), lambda j: (j, 0)),
    ]
    anywhere = pl.BlockSpec(memory_space=pl.ANY)
    in_vmem = pl.BlockSpec(memory_space=pltpu.VMEM)
    return pl.pallas_call(
        functools.partial(side_pipeline, odd, specs_in, specs_out, col_len // block_len),
        in_specs=[pl.BlockSpec(memory_space=pltpu.SMEM)] + [in_vmem] * 3 + [anywhere] * (2 + len(into)),
        out_specs=[anywhere] * len(specs_out),
        out_shape=[
            pltpu.HBM((col_len, 4 * hidden_width, row_len), jnp.bfloat16),
            pltpu.HBM(z_norm.shape, jnp.float32),
            pltpu.HBM(z_norm.shape, jnp.bfloat16),
            pltpu.HBM((hidden_width, col_len, row_len), jnp.float32),
            pltpu.HBM((col_len, row_len), jnp.float32),
        ],
        scratch_shapes=[
            pltpu.VMEM((4 * hidden_width, width), jnp.float32),
            pltpu.VMEM((4 * hidden_width, width), jnp.bfloat16),
            pltpu.VMEM((hidden_width, width), jnp.float32),
        ],
        input_output_aliases={6 + at: at for at in range(len(into))},
        name="side_work",
    )(lengths, weight_in, w_out, gain_out[None], z_norm, cotangent, *into)


def projection_grads(grad_ref, factor_ref):
    hidden_width, _, block_len, row_len = grad_ref.shape
    grads = grad_ref[...].astype(jnp.float32).reshape(2 * hidden_width, block_len, row_len)
    grads = jnp.swapaxes(grads, 0, 1)
    return [
        jnp.concatenate(
            [
                (grads[j] * factor_ref[j, : 2 * hidden_width].astype(jnp.float32)),
                (grads[j] * factor_ref[j, 2 * hidden_width :].astype(jnp.float32)),
            ],
            0,
        ).astype(jnp.bfloat16)
        for j in range(block_len)
    ]


def block_output_kernel(
    outer_ref, gate_ref, grad_proj_ref, cotangent_ref, norm_ref, w_out_ref, gain_ref,
    mixed_ref, grad_gate_ref, sum_out_ref, sum_gate_ref,
):
    hidden_width, block_len, row_len = outer_ref.shape
    width = norm_ref.shape[2]
    o_hat, _ = normalize(outer_ref[...].astype(jnp.float32), 0)
    o_hat = jnp.swapaxes(o_hat, 0, 1)
    grad_out = jnp.swapaxes(cotangent_ref[...].astype(jnp.float32), 0, 1)
    spread = gain_rows(gain_ref)
    normed, mixed = [], []
    for j in range(block_len):
        o_norm = (o_hat[j] * spread).astype(jnp.bfloat16)
        normed.append(o_norm)
        proj_out = lax.dot_general(
            o_norm, w_out_ref[...], (((0,), (0,)), ((), ())), preferred_element_type=jnp.float32
        )
        gate = gate_ref[j]
        mixed.append(gate * proj_out)
        grad_gate_ref[j] = (grad_out[j] * proj_out * gate * (1.0 - gate)).astype(jnp.bfloat16)
    mixed_ref[...] = jnp.swapaxes(jnp.stack(mixed, 0), 0, 1).astype(jnp.bfloat16)
    flat = (block_len * row_len, width)
    sum_out = jnp.dot(
        jnp.concatenate(normed, 1), grad_proj_ref[...].reshape(flat), preferred_element_type=jnp.float32
    )
    sum_gate = lax.dot_general(
        norm_ref[...].reshape(flat),
        grad_gate_ref[...].reshape(flat),
        (((0,), (0,)), ((), ())),
        preferred_element_type=jnp.float32,
    )

    @pl.when(pl.program_id(0) == 0)
    def _():
        sum_out_ref[...] = sum_out
        sum_gate_ref[...] = sum_gate

    @pl.when(pl.program_id(0) > 0)
    def _():
        sum_out_ref[...] += sum_out
        sum_gate_ref[...] += sum_gate


def block_output(outer_tile, gate, grad_proj, cotangent, z_norm, w_out, gain_out, block_len=16):
    hidden_width, col_len, row_len = outer_tile.shape
    width = z_norm.shape[2]
    by_pair = pl.BlockSpec((block_len, row_len, width), lambda j: (j, 0, 0))
    natural = pl.BlockSpec((row_len, block_len, width), lambda j: (0, j, 0))
    square = pl.BlockSpec((width, width), lambda j: (0, 0))
    return pl.pallas_call(
        block_output_kernel,
        grid=(col_len // block_len,),
        in_specs=[
            pl.BlockSpec((hidden_width, block_len, row_len), lambda j: (0, j, 0)),
            by_pair,
            by_pair,
            natural,
            by_pair,
            square,
            pl.BlockSpec((1, width), lambda j: (0, 0)),
        ],
        out_specs=[natural, by_pair, square, square],
        out_shape=[
            pltpu.HBM(cotangent.shape, jnp.bfloat16),
            pltpu.HBM(z_norm.shape, jnp.bfloat16),
            pltpu.HBM((width, width), jnp.float32),
            pltpu.HBM((width, width), jnp.float32),
        ],
        compiler_params=pltpu.CompilerParams(vmem_limit_bytes=48 << 20),
        name="block_output",
    )(outer_tile, gate, grad_proj, cotangent, z_norm, w_out, gain_out[None])


def weight_sums_kernel(grad_ref, factor_ref, norm_ref, gate_ref, out_ref, sum_ref, total_ref):
    hidden_width, _, block_len, row_len = grad_ref.shape
    width = norm_ref.shape[2]
    step = pl.program_id(0)
    grads = jnp.concatenate(projection_grads(grad_ref, factor_ref), 1)
    partial = jnp.dot(
        grads,
        norm_ref[...].reshape(block_len * row_len, width),
        preferred_element_type=jnp.float32,
    )

    @pl.when(step == 0)
    def _():
        total_ref[...] = partial

    @pl.when(step > 0)
    def _():
        total_ref[...] += partial

    @pl.when(step == pl.num_programs(0) - 1)
    def _():
        for side in range(2):
            for kind in range(2):
                rows = total_ref[
                    pl.ds(kind * 2 * hidden_width + side, hidden_width, stride=2), :
                ]
                at = (2 * side + kind) * width
                sum_ref[at : at + width] = rows.T
        sum_ref[4 * width : 5 * width] = gate_ref[...]
        sum_ref[5 * width : 6 * width] = out_ref[...]
        sum_ref[6 * width :] = jnp.zeros((2 * width, width), jnp.float32)


def weight_sums(grad_tiles, factors, z_norm, grad_w_gate, grad_w_out, block_len=16):
    hidden_width, _, col_len, row_len = grad_tiles.shape
    width = z_norm.shape[2]
    square = pl.BlockSpec((width, width), lambda j: (0, 0))
    return pl.pallas_call(
        weight_sums_kernel,
        grid=(col_len // block_len,),
        in_specs=[
            pl.BlockSpec((hidden_width, 2, block_len, row_len), lambda j: (0, 0, j, 0)),
            pl.BlockSpec((block_len, 4 * hidden_width, row_len), lambda j: (j, 0, 0)),
            pl.BlockSpec((block_len, row_len, width), lambda j: (j, 0, 0)),
            square,
            square,
        ],
        out_specs=pl.BlockSpec((8 * width, width), lambda j: (0, 0)),
        out_shape=jax.ShapeDtypeStruct((8 * width, width), jnp.float32),
        scratch_shapes=[pltpu.VMEM((4 * hidden_width, width), jnp.float32)],
        name="weight_sums",
    )(grad_tiles, factors, z_norm, grad_w_gate, grad_w_out)


def pair_grad_kernel(
    pair_ref, grad_ref, factor_ref, gate_ref, weight_ref, w_gate_ref, gain_ref, _, out_ref
):
    block_len = pair_ref.shape[1]
    z_hat, z_inverse = layer_norm(jnp.swapaxes(pair_ref[...].astype(jnp.float32), 0, 1))
    grads = projection_grads(grad_ref, factor_ref)
    grad_norm = []
    for j in range(block_len):
        total = jnp.dot(weight_ref[...], grads[j], preferred_element_type=jnp.float32)
        total += lax.dot_general(
            w_gate_ref[...], gate_ref[j], (((1,), (1,)), ((), ())), preferred_element_type=jnp.float32
        )
        grad_norm.append(total.T)
    grad_hat = jnp.stack(grad_norm, 0) * gain_ref[...]
    grad_pair = normalize_back(grad_hat, z_hat, z_inverse, -1)
    out_ref[...] = jnp.swapaxes(grad_pair, 0, 1).astype(jnp.bfloat16)


def pair_grad(half, into, pair_rep, grad_tiles, factors, grad_gate, w_tri, w_gate, gain, block_len=16):
    row_len, col_len, width = pair_rep.shape
    hidden_width = grad_tiles.shape[0]
    steps = col_len // block_len // 2
    first = half * steps
    return pl.pallas_call(
        pair_grad_kernel,
        grid=(steps,),
        in_specs=[
            pl.BlockSpec((row_len, block_len, width), lambda j: (0, first + j, 0)),
            pl.BlockSpec((hidden_width, 2, block_len, row_len), lambda j: (0, 0, first + j, 0)),
            pl.BlockSpec((block_len, 4 * hidden_width, row_len), lambda j: (first + j, 0, 0)),
            pl.BlockSpec((block_len, row_len, width), lambda j: (first + j, 0, 0)),
            pl.BlockSpec(w_tri.shape, lambda j: (0, 0)),
            pl.BlockSpec(w_gate.shape, lambda j: (0, 0)),
            pl.BlockSpec((1, width), lambda j: (0, 0)),
            pl.BlockSpec(memory_space=pl.ANY),
        ],
        out_specs=pl.BlockSpec((row_len, block_len, width), lambda j: (0, first + j, 0)),
        out_shape=jax.ShapeDtypeStruct(pair_rep.shape, jnp.bfloat16),
        input_output_aliases={7: 0},
        name="pair_grad",
    )(pair_rep, grad_tiles, factors, grad_gate, w_tri, w_gate, gain[None], into)


def finish_kernel(total_ref, w_in_ref, w_out_ref, g_in_ref, g_out_ref, gw_in_ref, gw_out_ref, gg_in_ref, gg_out_ref):
    width = gw_out_ref.shape[0]
    blocks = gw_in_ref.shape[1] // width
    along_in = jnp.zeros((width, 1), jnp.float32)
    for block in range(blocks):
        part = total_ref[block * width : (block + 1) * width] / N
        at = slice(block * width, (block + 1) * width)
        gw_in_ref[:, at] = part
        along_in += jnp.sum(part * w_in_ref[:, at].astype(jnp.float32), axis=1, keepdims=True)
    part = total_ref[blocks * width : (blocks + 1) * width] / N
    gw_out_ref[...] = part
    along_out = jnp.sum(part * w_out_ref[...].astype(jnp.float32), axis=1, keepdims=True)
    gg_in_ref[...] = jnp.broadcast_to(along_in, (width, width)).T[:1] / g_in_ref[...]
    gg_out_ref[...] = jnp.broadcast_to(along_out, (width, width)).T[:1] / g_out_ref[...]


def finish(totals, weight_in, weight_out, gain_in, gain_out):
    row = jax.ShapeDtypeStruct((1, gain_in.shape[0]), jnp.float32)
    grads = pl.pallas_call(
        finish_kernel,
        out_shape=[
            jax.ShapeDtypeStruct(weight_in.shape, jnp.float32),
            jax.ShapeDtypeStruct(weight_out.shape, jnp.float32),
            row,
            row,
        ],
        compiler_params=pltpu.CompilerParams(vmem_limit_bytes=16 << 20),
        name="finish",
    )(totals, weight_in, weight_out, gain_in[None], gain_out[None])
    return grads[0], grads[1], grads[2][0], grads[3][0]


def outer_grad_kernel(outer_ref, back_ref, mean_ref, grad_ref):
    hidden_width = outer_ref.shape[0]
    zero = jnp.zeros(mean_ref.shape, jnp.float32)

    def over_channels(step, start):
        return lax.fori_loop(0, hidden_width, step, start, unroll=16)

    mean = over_channels(lambda h, run: run + outer_ref[h].astype(jnp.float32), zero) / hidden_width

    def products(h, run):
        centred = outer_ref[h].astype(jnp.float32) - mean
        return run[0] + centred * centred, run[1] + centred * back_ref[h]

    square, cross = over_channels(products, (zero, zero))
    inverse = lax.rsqrt(square / hidden_width + epsilon)
    slope = inverse * inverse * inverse * (cross / hidden_width)
    offset = inverse * mean_ref[...]

    def write(h, run):
        centred = outer_ref[h].astype(jnp.float32) - mean
        grad_ref[h] = (inverse * back_ref[h] - offset - centred * slope).astype(jnp.bfloat16)
        return run

    over_channels(write, 0)


def outer_grad(outer_tile, back, back_mean, block_len=16):
    hidden_width, col_len, row_len = outer_tile.shape
    whole = pl.BlockSpec((hidden_width, block_len, row_len), lambda j: (0, j, 0))
    return pl.pallas_call(
        outer_grad_kernel,
        grid=(col_len // block_len,),
        in_specs=[whole, whole, pl.BlockSpec((block_len, row_len), lambda j: (j, 0))],
        out_specs=whole,
        out_shape=pltpu.HBM(outer_tile.shape, jnp.bfloat16),
        compiler_params=pltpu.CompilerParams(vmem_limit_bytes=48 << 20),
        name="outer_grad",
    )(outer_tile, back, back_mean)


def on_device(pair_rep, cotangent, lengths, weight_in, weight_out, gain_in, gain_out):
    rows_n = lax.axis_size("row")
    cols_n = lax.axis_size("col")
    devices = rows_n * cols_n
    row_len = pair_rep.shape[1]
    col_len = pair_rep.shape[2]
    width = pair_rep.shape[3]
    hidden_width = weight_out.shape[0]
    share = hidden_width // devices

    pair_tiles, z_norm = project(lengths, pair_rep[0], weight_in, gain_in)
    side_args = (lengths, weight_in, weight_out, gain_out, z_norm, cotangent[0])
    side = side_work(1, (), *side_args)
    pair_tiles, *side = lax.optimization_barrier((pair_tiles, *side))
    pair_ch = exchange(pair_tiles).reshape(devices, share, 2, col_len, row_len)
    outer_ch = triangle(pair_ch, rows_n, cols_n)
    outer_ch, *side = lax.optimization_barrier((outer_ch, *side))
    outer_tile = exchange(outer_ch.reshape(hidden_width, col_len, row_len))
    side = side_work(0, tuple(side), *side_args)
    outer_tile, *side = lax.optimization_barrier((outer_tile, *side))
    factors, gate, grad_proj, back, back_mean = side
    grad_outer = outer_grad(outer_tile, back, back_mean)
    grad_ch = exchange(grad_outer).reshape(devices, share, col_len, row_len)

    mixed, grad_gate, grad_w_out, grad_w_gate = block_output(
        outer_tile, gate, grad_proj, cotangent[0], z_norm, weight_out, gain_out
    )
    grad_ch, mixed, grad_gate, grad_w_gate, grad_w_out = lax.optimization_barrier(
        (grad_ch, mixed, grad_gate, grad_w_gate, grad_w_out)
    )
    grad_parts = triangle_back(pair_ch, grad_ch, rows_n, cols_n)
    grad_tiles = exchange(grad_parts.reshape(hidden_width, 2, col_len, row_len))
    grad_tiles, late_weight = lax.optimization_barrier((grad_tiles, weight_in))
    w_tri = late_weight[:, : 4 * hidden_width].reshape(width, 2, 2, hidden_width)
    w_tri = w_tri.transpose(0, 2, 3, 1).reshape(width, 4 * hidden_width)
    w_gate = late_weight[:, 4 * hidden_width :]
    sums = weight_sums(grad_tiles, factors, z_norm, grad_w_gate, grad_w_out)
    pieces = sums.reshape(lax.axis_size(ALL), -1, width)
    arrived = lax.all_to_all(pieces, ALL, split_axis=0, concat_axis=0, tiled=True)
    pair_parts = (pair_rep[0], grad_tiles, factors, grad_gate, w_tri, w_gate, gain_in)
    grad_pair = pair_grad(0, z_norm.reshape(pair_rep.shape[1:]), *pair_parts)
    arrived, grad_pair = lax.optimization_barrier((arrived, grad_pair))
    spread = jnp.broadcast_to(jnp.sum(arrived, axis=0, keepdims=True), pieces.shape)
    totals = lax.all_to_all(spread, ALL, split_axis=0, concat_axis=0, tiled=True)
    grad_pair = pair_grad(1, grad_pair, *pair_parts)
    grad_w_in, grad_w_out, grad_g_in, grad_g_out = finish(
        totals.reshape(sums.shape), weight_in, weight_out, gain_in, gain_out
    )
    return (mixed[None], grad_pair[None], grad_w_in, grad_w_out, grad_g_in, grad_g_out)


def solution(mesh):
    return jax.shard_map(
        on_device,
        mesh=mesh,
        in_specs=(
            P("grp", "row", "col", None),
            P("grp", "row", "col", None),
            P(),
            P(),
            P(),
            P(),
            P(),
        ),
        out_specs=(P("grp", "row", "col", None), P("grp", "row", "col", None), P(), P(), P(), P()),
        check_vma=False,
    )
```

```python
import functools

import jax
import jax.numpy as jnp
from jax import lax
from jax.experimental import pallas as pl
from jax.experimental.pallas import tpu as pltpu
from jax.sharding import PartitionSpec as P

N = 512
ALL = ("grp", "row", "col")
TILE = ("row", "col")
STAGGER_NS = 7000


epsilon = 1e-05


def normalize(values, along):
    centred = values - jnp.mean(values, axis=along, keepdims=True)
    inverse = lax.rsqrt(jnp.mean(centred * centred, axis=along, keepdims=True) + epsilon)
    return (centred * inverse, inverse)


def normalize_back(grad_hat, normed, inverse, along):
    first_mean = jnp.mean(grad_hat, axis=along, keepdims=True)
    second_mean = jnp.mean(grad_hat * normed, axis=along, keepdims=True)
    return inverse * (grad_hat - first_mean - normed * second_mean)


def exchange(tiles):
    return lax.all_to_all(tiles, TILE, split_axis=0, concat_axis=0, tiled=True)


def forward_kernel(rows_n, cols_n, pair_ref, out_ref, left_ref, right_ref):
    col_len, row_len = pair_ref.shape[3], pair_ref.shape[4]
    for r in range(rows_n):
        for c in range(cols_n):
            at = (pl.ds(c * col_len, col_len), pl.ds(r * row_len, row_len))
            left_ref[at] = pair_ref[r * cols_n + c, 0, 0]
            right_ref[at] = pair_ref[r * cols_n + c, 0, 1]
    outer = lax.dot_general(
        right_ref[...], left_ref[...], (((0,), (0,)), ((), ())), preferred_element_type=jnp.float32
    ).astype(jnp.bfloat16)
    for r in range(rows_n):
        for c in range(cols_n):
            out_ref[r * cols_n + c, 0] = outer[
                c * col_len : (c + 1) * col_len, r * row_len : (r + 1) * row_len
            ]


def backward_kernel(rows_n, cols_n, pair_ref, grad_ref, out_ref, left_ref, right_ref, outer_ref):
    col_len, row_len = pair_ref.shape[3], pair_ref.shape[4]
    for r in range(rows_n):
        for c in range(cols_n):
            at = (pl.ds(c * col_len, col_len), pl.ds(r * row_len, row_len))
            left_ref[at] = pair_ref[r * cols_n + c, 0, 0]
            right_ref[at] = pair_ref[r * cols_n + c, 0, 1]
            outer_ref[at] = grad_ref[r * cols_n + c, 0]
    grad_left = lax.dot_general(
        right_ref[...], outer_ref[...], (((1,), (0,)), ((), ())), preferred_element_type=jnp.float32
    ).astype(jnp.bfloat16)
    grad_right = lax.dot_general(
        left_ref[...], outer_ref[...], (((1,), (1,)), ((), ())), preferred_element_type=jnp.float32
    ).astype(jnp.bfloat16)
    for r in range(rows_n):
        for c in range(cols_n):
            at = (slice(c * col_len, (c + 1) * col_len), slice(r * row_len, (r + 1) * row_len))
            out_ref[r * cols_n + c, 0, 0] = grad_left[at]
            out_ref[r * cols_n + c, 0, 1] = grad_right[at]


def triangle(pair_ch, rows_n, cols_n):
    devices, share, _, col_len, row_len = pair_ch.shape
    side = cols_n * col_len
    return pl.pallas_call(
        functools.partial(forward_kernel, rows_n, cols_n),
        grid=(share,),
        in_specs=[pl.BlockSpec((devices, 1, 2, col_len, row_len), lambda h: (0, h, 0, 0, 0))],
        out_specs=pl.BlockSpec((devices, 1, col_len, row_len), lambda h: (0, h, 0, 0)),
        out_shape=jax.ShapeDtypeStruct((devices, share, col_len, row_len), jnp.bfloat16),
        scratch_shapes=[pltpu.VMEM((side, side), jnp.bfloat16)] * 2,
        name="triangle_forward",
    )(pair_ch)


def triangle_back(pair_ch, grad_ch, rows_n, cols_n):
    devices, share, _, col_len, row_len = pair_ch.shape
    side = cols_n * col_len
    return pl.pallas_call(
        functools.partial(backward_kernel, rows_n, cols_n),
        grid=(share,),
        in_specs=[
            pl.BlockSpec((devices, 1, 2, col_len, row_len), lambda h: (0, h, 0, 0, 0)),
            pl.BlockSpec((devices, 1, col_len, row_len), lambda h: (0, h, 0, 0)),
        ],
        out_specs=pl.BlockSpec((devices, 1, 2, col_len, row_len), lambda h: (0, h, 0, 0, 0)),
        out_shape=pltpu.HBM(pair_ch.shape, jnp.bfloat16),
        scratch_shapes=[pltpu.VMEM((side, side), jnp.bfloat16)] * 3,
        compiler_params=pltpu.CompilerParams(vmem_limit_bytes=48 << 20),
        name="triangle_backward",
    )(pair_ch, grad_ch)


def layer_norm(values):
    centred = values - jnp.mean(values, axis=-1, keepdims=True)
    inverse = lax.rsqrt(jnp.mean(centred * centred, axis=-1, keepdims=True) + epsilon)
    return centred * inverse, inverse


def tile_inside(lengths_ref, row_len, block_len):
    length = lengths_ref[lax.axis_index("grp")]
    row_start = lax.axis_index("row") * row_len
    col_start = (lax.axis_index("col") * pl.num_programs(0) + pl.program_id(0)) * block_len
    row_in = row_start + lax.broadcasted_iota(jnp.int32, (1, row_len), 1) < length
    return [
        jnp.where(row_in & (col_start + j < length), 1.0, 0.0).astype(jnp.float32)
        for j in range(block_len)
    ]


def project_kernel(lengths_ref, pair_ref, weight_ref, gain_ref, tile_ref, norm_ref, rows_ref):
    row_len, block_len, _ = pair_ref.shape
    hidden_width = tile_ref.shape[0]
    first = pl.program_id(0) == 0

    @pl.when(first)
    def _():
        for at, source in enumerate((0, 2, 1, 3)):
            part = weight_ref[:, source * hidden_width : (source + 1) * hidden_width]
            rows_ref[at * hidden_width : (at + 1) * hidden_width] = part.astype(jnp.float32).T.astype(
                jnp.bfloat16
            )

    normed, _ = layer_norm(jnp.swapaxes(pair_ref[...].astype(jnp.float32), 0, 1))
    normed = (normed * gain_ref[...]).astype(jnp.bfloat16)
    norm_ref[...] = normed
    inside = tile_inside(lengths_ref, row_len, block_len)
    gated = []
    for j in range(block_len):
        projected = lax.dot_general(
            rows_ref[...], normed[j], (((1,), (1,)), ((), ())), preferred_element_type=jnp.float32
        )
        sig = jax.nn.sigmoid(projected[2 * hidden_width :])
        gated.append(projected[: 2 * hidden_width] * sig * inside[j])
    gated = jnp.swapaxes(jnp.stack(gated, 0), 0, 1).astype(jnp.bfloat16)
    tile_ref[:, 0] = gated[:hidden_width]
    tile_ref[:, 1] = gated[hidden_width:]


def project(lengths, pair_rep, weight_in, gain, block_len=16):
    row_len, col_len, width = pair_rep.shape
    hidden_width = (weight_in.shape[1] - width) // 4
    return pl.pallas_call(
        project_kernel,
        grid=(col_len // block_len,),
        in_specs=[
            pl.BlockSpec(memory_space=pltpu.SMEM),
            pl.BlockSpec((row_len, block_len, width), lambda j: (0, j, 0)),
            pl.BlockSpec(weight_in.shape, lambda j: (0, 0)),
            pl.BlockSpec((1, width), lambda j: (0, 0)),
        ],
        out_specs=[
            pl.BlockSpec((hidden_width, 2, block_len, row_len), lambda j: (0, 0, j, 0)),
            pl.BlockSpec((block_len, row_len, width), lambda j: (j, 0, 0)),
        ],
        out_shape=[
            jax.ShapeDtypeStruct((hidden_width, 2, col_len, row_len), jnp.bfloat16),
            jax.ShapeDtypeStruct((col_len, row_len, width), jnp.bfloat16),
        ],
        scratch_shapes=[pltpu.VMEM((4 * hidden_width, width), jnp.bfloat16)],
        name="project",
    )(lengths, pair_rep, weight_in, gain[None])


def side_kernel(
    lengths_ref,
    weight_ref,
    w_gate_ref,
    w_out_ref,
    gain_ref,
    norm_ref,
    cotangent_ref,
    factor_ref,
    gate_ref,
    grad_proj_ref,
    back_ref,
    mean_ref,
):
    block_len, row_len, width = norm_ref.shape
    half = weight_ref.shape[0] // 2
    inside = tile_inside(lengths_ref, row_len, block_len)
    grad_out = jnp.swapaxes(cotangent_ref[...].astype(jnp.float32), 0, 1)
    length = lengths_ref[lax.axis_index("grp")]
    row_at = lax.axis_index("row") * row_len + lax.broadcasted_iota(jnp.int32, (row_len, 1), 0)
    col_start = (lax.axis_index("col") * pl.num_programs(0) + pl.program_id(0)) * block_len
    backs = []
    for j in range(block_len):
        projected = lax.dot_general(
            weight_ref[...], norm_ref[j], (((1,), (1,)), ((), ())), preferred_element_type=jnp.float32
        )
        sig = jax.nn.sigmoid(projected[half:])
        kept = sig * inside[j]
        factor_ref[j, :half] = kept.astype(jnp.bfloat16)
        factor_ref[j, half:] = (projected[:half] * kept * (1.0 - sig)).astype(jnp.bfloat16)
        here = jnp.where((row_at < length) & (col_start + j < length), 1.0, 0.0)
        gate_pre = jnp.dot(norm_ref[j], w_gate_ref[...], preferred_element_type=jnp.float32)
        gate = jax.nn.sigmoid(gate_pre) * here
        gate_ref[j] = gate
        grad_proj = (grad_out[j] * gate).astype(jnp.bfloat16)
        grad_proj_ref[j] = grad_proj
        back = gain_ref[...] * lax.dot_general(
            w_out_ref[...], grad_proj, (((1,), (1,)), ((), ())), preferred_element_type=jnp.float32
        )
        mean_ref[j : j + 1] = jnp.mean(back, axis=0, keepdims=True)
        backs.append(back)
    back_ref[...] = jnp.swapaxes(jnp.stack(backs, 0), 0, 1)


def gain_rows(gain_ref):
    width = gain_ref.shape[1]
    return jnp.broadcast_to(gain_ref[...], (width, width)).T


def side_pipeline(odd, specs_in, specs_out, steps, lengths_ref, weight_ref, w_out_ref, gain_ref, *refs):
    *refs, wide_ref, rows_ref, spread_ref = refs
    inputs, outputs = refs[: len(specs_in)], refs[-len(specs_out) :]
    width = w_out_ref.shape[0]

    @pl.when(lax.axis_index("grp") % 2 == odd)
    def _():
        if odd and STAGGER_NS:
            pl.delay(STAGGER_NS)
        for side in range(2):
            for kind in range(2):
                source = (2 * side + kind) * width
                part = weight_ref[:, source : source + width].astype(jnp.float32).T
                wide_ref[pl.ds(kind * 2 * width + side, width, stride=2), :] = part
        rows_ref[...] = wide_ref[...].astype(jnp.bfloat16)
        spread_ref[...] = gain_rows(gain_ref)
        w_gate_ref = weight_ref.at[:, 4 * width :]
        pltpu.emit_pipeline(
            functools.partial(side_kernel, lengths_ref, rows_ref, w_gate_ref, w_out_ref, spread_ref),
            grid=(steps,),
            in_specs=specs_in,
            out_specs=specs_out,
        )(*inputs, *outputs)


def side_work(odd, into, lengths, weight_in, w_out, gain_out, z_norm, cotangent, block_len=16):
    col_len, row_len, width = z_norm.shape
    hidden_width = w_out.shape[0]
    by_pair = pl.BlockSpec((block_len, row_len, width), lambda j: (j, 0, 0))
    specs_in = [by_pair, pl.BlockSpec((row_len, block_len, width), lambda j: (0, j, 0))]
    specs_out = [
        pl.BlockSpec((block_len, 4 * hidden_width, row_len), lambda j: (j, 0, 0)),
        by_pair,
        by_pair,
        pl.BlockSpec((hidden_width, block_len, row_len), lambda j: (0, j, 0)),
        pl.BlockSpec((block_len, row_len), lambda j: (j, 0)),
    ]
    anywhere = pl.BlockSpec(memory_space=pl.ANY)
    in_vmem = pl.BlockSpec(memory_space=pltpu.VMEM)
    return pl.pallas_call(
        functools.partial(side_pipeline, odd, specs_in, specs_out, col_len // block_len),
        in_specs=[pl.BlockSpec(memory_space=pltpu.SMEM)] + [in_vmem] * 3 + [anywhere] * (2 + len(into)),
        out_specs=[anywhere] * len(specs_out),
        out_shape=[
            pltpu.HBM((col_len, 4 * hidden_width, row_len), jnp.bfloat16),
            pltpu.HBM(z_norm.shape, jnp.float32),
            pltpu.HBM(z_norm.shape, jnp.bfloat16),
            pltpu.HBM((hidden_width, col_len, row_len), jnp.float32),
            pltpu.HBM((col_len, row_len), jnp.float32),
        ],
        scratch_shapes=[
            pltpu.VMEM((4 * hidden_width, width), jnp.float32),
            pltpu.VMEM((4 * hidden_width, width), jnp.bfloat16),
            pltpu.VMEM((hidden_width, width), jnp.float32),
        ],
        input_output_aliases={6 + at: at for at in range(len(into))},
        name="side_work",
    )(lengths, weight_in, w_out, gain_out[None], z_norm, cotangent, *into)


def projection_grads(grad_ref, factor_ref):
    hidden_width, _, block_len, row_len = grad_ref.shape
    grads = grad_ref[...].astype(jnp.float32).reshape(2 * hidden_width, block_len, row_len)
    grads = jnp.swapaxes(grads, 0, 1)
    return [
        jnp.concatenate(
            [
                (grads[j] * factor_ref[j, : 2 * hidden_width].astype(jnp.float32)),
                (grads[j] * factor_ref[j, 2 * hidden_width :].astype(jnp.float32)),
            ],
            0,
        ).astype(jnp.bfloat16)
        for j in range(block_len)
    ]


def block_output_kernel(
    outer_ref, gate_ref, grad_proj_ref, cotangent_ref, norm_ref, w_out_ref, gain_ref,
    mixed_ref, grad_gate_ref, sum_out_ref, sum_gate_ref,
):
    hidden_width, block_len, row_len = outer_ref.shape
    width = norm_ref.shape[2]
    o_hat, _ = normalize(outer_ref[...].astype(jnp.float32), 0)
    o_hat = jnp.swapaxes(o_hat, 0, 1)
    grad_out = jnp.swapaxes(cotangent_ref[...].astype(jnp.float32), 0, 1)
    spread = gain_rows(gain_ref)
    normed, mixed = [], []
    for j in range(block_len):
        o_norm = (o_hat[j] * spread).astype(jnp.bfloat16)
        normed.append(o_norm)
        proj_out = lax.dot_general(
            o_norm, w_out_ref[...], (((0,), (0,)), ((), ())), preferred_element_type=jnp.float32
        )
        gate = gate_ref[j]
        mixed.append(gate * proj_out)
        grad_gate_ref[j] = (grad_out[j] * proj_out * gate * (1.0 - gate)).astype(jnp.bfloat16)
    mixed_ref[...] = jnp.swapaxes(jnp.stack(mixed, 0), 0, 1).astype(jnp.bfloat16)
    flat = (block_len * row_len, width)
    sum_out = jnp.dot(
        jnp.concatenate(normed, 1), grad_proj_ref[...].reshape(flat), preferred_element_type=jnp.float32
    )
    sum_gate = lax.dot_general(
        norm_ref[...].reshape(flat),
        grad_gate_ref[...].reshape(flat),
        (((0,), (0,)), ((), ())),
        preferred_element_type=jnp.float32,
    )

    @pl.when(pl.program_id(0) == 0)
    def _():
        sum_out_ref[...] = sum_out
        sum_gate_ref[...] = sum_gate

    @pl.when(pl.program_id(0) > 0)
    def _():
        sum_out_ref[...] += sum_out
        sum_gate_ref[...] += sum_gate


def block_output(outer_tile, gate, grad_proj, cotangent, z_norm, w_out, gain_out, block_len=16):
    hidden_width, col_len, row_len = outer_tile.shape
    width = z_norm.shape[2]
    by_pair = pl.BlockSpec((block_len, row_len, width), lambda j: (j, 0, 0))
    natural = pl.BlockSpec((row_len, block_len, width), lambda j: (0, j, 0))
    square = pl.BlockSpec((width, width), lambda j: (0, 0))
    return pl.pallas_call(
        block_output_kernel,
        grid=(col_len // block_len,),
        in_specs=[
            pl.BlockSpec((hidden_width, block_len, row_len), lambda j: (0, j, 0)),
            by_pair,
            by_pair,
            natural,
            by_pair,
            square,
            pl.BlockSpec((1, width), lambda j: (0, 0)),
        ],
        out_specs=[natural, by_pair, square, square],
        out_shape=[
            pltpu.HBM(cotangent.shape, jnp.bfloat16),
            pltpu.HBM(z_norm.shape, jnp.bfloat16),
            pltpu.HBM((width, width), jnp.float32),
            pltpu.HBM((width, width), jnp.float32),
        ],
        compiler_params=pltpu.CompilerParams(vmem_limit_bytes=48 << 20),
        name="block_output",
    )(outer_tile, gate, grad_proj, cotangent, z_norm, w_out, gain_out[None])


def weight_sums_kernel(grad_ref, factor_ref, norm_ref, gate_ref, out_ref, sum_ref, total_ref):
    hidden_width, _, block_len, row_len = grad_ref.shape
    width = norm_ref.shape[2]
    step = pl.program_id(0)
    grads = jnp.concatenate(projection_grads(grad_ref, factor_ref), 1)
    partial = jnp.dot(
        grads,
        norm_ref[...].reshape(block_len * row_len, width),
        preferred_element_type=jnp.float32,
    )

    @pl.when(step == 0)
    def _():
        total_ref[...] = partial

    @pl.when(step > 0)
    def _():
        total_ref[...] += partial

    @pl.when(step == pl.num_programs(0) - 1)
    def _():
        for side in range(2):
            for kind in range(2):
                rows = total_ref[
                    pl.ds(kind * 2 * hidden_width + side, hidden_width, stride=2), :
                ]
                at = (2 * side + kind) * width
                sum_ref[at : at + width] = rows.T
        sum_ref[4 * width : 5 * width] = gate_ref[...]
        sum_ref[5 * width : 6 * width] = out_ref[...]
        sum_ref[6 * width :] = jnp.zeros((2 * width, width), jnp.float32)


def weight_sums(grad_tiles, factors, z_norm, grad_w_gate, grad_w_out, block_len=16):
    hidden_width, _, col_len, row_len = grad_tiles.shape
    width = z_norm.shape[2]
    square = pl.BlockSpec((width, width), lambda j: (0, 0))
    return pl.pallas_call(
        weight_sums_kernel,
        grid=(col_len // block_len,),
        in_specs=[
            pl.BlockSpec((hidden_width, 2, block_len, row_len), lambda j: (0, 0, j, 0)),
            pl.BlockSpec((block_len, 4 * hidden_width, row_len), lambda j: (j, 0, 0)),
            pl.BlockSpec((block_len, row_len, width), lambda j: (j, 0, 0)),
            square,
            square,
        ],
        out_specs=pl.BlockSpec((8 * width, width), lambda j: (0, 0)),
        out_shape=pltpu.HBM((8 * width, width), jnp.float32),
        scratch_shapes=[pltpu.VMEM((4 * hidden_width, width), jnp.float32)],
        compiler_params=pltpu.CompilerParams(vmem_limit_bytes=46 << 20),
        name="weight_sums",
    )(grad_tiles, factors, z_norm, grad_w_gate, grad_w_out)


def pair_grad_kernel(
    pair_ref, grad_ref, factor_ref, gate_ref, weight_ref, w_gate_ref, gain_ref, _, out_ref
):
    block_len = pair_ref.shape[1]
    z_hat, z_inverse = layer_norm(jnp.swapaxes(pair_ref[...].astype(jnp.float32), 0, 1))
    grads = projection_grads(grad_ref, factor_ref)
    grad_norm = []
    for j in range(block_len):
        total = jnp.dot(weight_ref[...], grads[j], preferred_element_type=jnp.float32)
        total += lax.dot_general(
            w_gate_ref[...], gate_ref[j], (((1,), (1,)), ((), ())), preferred_element_type=jnp.float32
        )
        grad_norm.append(total.T)
    grad_hat = jnp.stack(grad_norm, 0) * gain_ref[...]
    grad_pair = normalize_back(grad_hat, z_hat, z_inverse, -1)
    out_ref[...] = jnp.swapaxes(grad_pair, 0, 1).astype(jnp.bfloat16)


def pair_grad(half, into, pair_rep, grad_tiles, factors, grad_gate, w_tri, w_gate, gain, block_len=16):
    row_len, col_len, width = pair_rep.shape
    hidden_width = grad_tiles.shape[0]
    steps = col_len // block_len // 2
    first = half * steps
    return pl.pallas_call(
        pair_grad_kernel,
        grid=(steps,),
        in_specs=[
            pl.BlockSpec((row_len, block_len, width), lambda j: (0, first + j, 0)),
            pl.BlockSpec((hidden_width, 2, block_len, row_len), lambda j: (0, 0, first + j, 0)),
            pl.BlockSpec((block_len, 4 * hidden_width, row_len), lambda j: (first + j, 0, 0)),
            pl.BlockSpec((block_len, row_len, width), lambda j: (first + j, 0, 0)),
            pl.BlockSpec(w_tri.shape, lambda j: (0, 0)),
            pl.BlockSpec(w_gate.shape, lambda j: (0, 0)),
            pl.BlockSpec((1, width), lambda j: (0, 0)),
            pl.BlockSpec(memory_space=pl.ANY),
        ],
        out_specs=pl.BlockSpec((row_len, block_len, width), lambda j: (0, first + j, 0)),
        out_shape=jax.ShapeDtypeStruct(pair_rep.shape, jnp.bfloat16),
        input_output_aliases={7: 0},
        name="pair_grad",
    )(pair_rep, grad_tiles, factors, grad_gate, w_tri, w_gate, gain[None], into)


def finish_kernel(total_ref, w_in_ref, w_out_ref, g_in_ref, g_out_ref, gw_in_ref, gw_out_ref, gg_in_ref, gg_out_ref):
    width = gw_out_ref.shape[0]
    blocks = gw_in_ref.shape[1] // width
    along_in = jnp.zeros((width, 1), jnp.float32)
    for block in range(blocks):
        part = total_ref[block * width : (block + 1) * width] / N
        at = slice(block * width, (block + 1) * width)
        gw_in_ref[:, at] = part
        along_in += jnp.sum(part * w_in_ref[:, at].astype(jnp.float32), axis=1, keepdims=True)
    part = total_ref[blocks * width : (blocks + 1) * width] / N
    gw_out_ref[...] = part
    along_out = jnp.sum(part * w_out_ref[...].astype(jnp.float32), axis=1, keepdims=True)
    gg_in_ref[...] = jnp.broadcast_to(along_in, (width, width)).T[:1] / g_in_ref[...]
    gg_out_ref[...] = jnp.broadcast_to(along_out, (width, width)).T[:1] / g_out_ref[...]


def finish(totals, weight_in, weight_out, gain_in, gain_out):
    row = jax.ShapeDtypeStruct((1, gain_in.shape[0]), jnp.float32)
    grads = pl.pallas_call(
        finish_kernel,
        out_shape=[
            jax.ShapeDtypeStruct(weight_in.shape, jnp.float32),
            jax.ShapeDtypeStruct(weight_out.shape, jnp.float32),
            row,
            row,
        ],
        compiler_params=pltpu.CompilerParams(vmem_limit_bytes=16 << 20),
        name="finish",
    )(totals, weight_in, weight_out, gain_in[None], gain_out[None])
    return grads[0], grads[1], grads[2][0], grads[3][0]


def outer_grad_kernel(outer_ref, back_ref, mean_ref, grad_ref):
    hidden_width = outer_ref.shape[0]
    zero = jnp.zeros(mean_ref.shape, jnp.float32)

    def over_channels(step, start):
        return lax.fori_loop(0, hidden_width, step, start, unroll=16)

    mean = over_channels(lambda h, run: run + outer_ref[h].astype(jnp.float32), zero) / hidden_width

    def products(h, run):
        centred = outer_ref[h].astype(jnp.float32) - mean
        return run[0] + centred * centred, run[1] + centred * back_ref[h]

    square, cross = over_channels(products, (zero, zero))
    inverse = lax.rsqrt(square / hidden_width + epsilon)
    slope = inverse * inverse * inverse * (cross / hidden_width)
    offset = inverse * mean_ref[...]

    def write(h, run):
        centred = outer_ref[h].astype(jnp.float32) - mean
        grad_ref[h] = (inverse * back_ref[h] - offset - centred * slope).astype(jnp.bfloat16)
        return run

    over_channels(write, 0)


def outer_grad(outer_tile, back, back_mean, block_len=16):
    hidden_width, col_len, row_len = outer_tile.shape
    whole = pl.BlockSpec((hidden_width, block_len, row_len), lambda j: (0, j, 0))
    return pl.pallas_call(
        outer_grad_kernel,
        grid=(col_len // block_len,),
        in_specs=[whole, whole, pl.BlockSpec((block_len, row_len), lambda j: (j, 0))],
        out_specs=whole,
        out_shape=pltpu.HBM(outer_tile.shape, jnp.bfloat16),
        compiler_params=pltpu.CompilerParams(vmem_limit_bytes=48 << 20),
        name="outer_grad",
    )(outer_tile, back, back_mean)


def on_device(pair_rep, cotangent, lengths, weight_in, weight_out, gain_in, gain_out):
    rows_n = lax.axis_size("row")
    cols_n = lax.axis_size("col")
    devices = rows_n * cols_n
    row_len = pair_rep.shape[1]
    col_len = pair_rep.shape[2]
    width = pair_rep.shape[3]
    hidden_width = weight_out.shape[0]
    share = hidden_width // devices

    pair_tiles, z_norm = project(lengths, pair_rep[0], weight_in, gain_in)
    side_args = (lengths, weight_in, weight_out, gain_out, z_norm, cotangent[0])
    side = side_work(1, (), *side_args)
    pair_tiles, *side = lax.optimization_barrier((pair_tiles, *side))
    pair_ch = exchange(pair_tiles).reshape(devices, share, 2, col_len, row_len)
    outer_ch = triangle(pair_ch, rows_n, cols_n)
    outer_ch, *side = lax.optimization_barrier((outer_ch, *side))
    outer_tile = exchange(outer_ch.reshape(hidden_width, col_len, row_len))
    side = side_work(0, tuple(side), *side_args)
    outer_tile, *side = lax.optimization_barrier((outer_tile, *side))
    factors, gate, grad_proj, back, back_mean = side
    grad_outer = outer_grad(outer_tile, back, back_mean)
    grad_ch = exchange(grad_outer).reshape(devices, share, col_len, row_len)

    mixed, grad_gate, grad_w_out, grad_w_gate = block_output(
        outer_tile, gate, grad_proj, cotangent[0], z_norm, weight_out, gain_out
    )
    grad_ch, mixed, grad_gate, grad_w_gate, grad_w_out = lax.optimization_barrier(
        (grad_ch, mixed, grad_gate, grad_w_gate, grad_w_out)
    )
    grad_parts = triangle_back(pair_ch, grad_ch, rows_n, cols_n)
    grad_tiles = exchange(grad_parts.reshape(hidden_width, 2, col_len, row_len))
    grad_tiles, late_weight = lax.optimization_barrier((grad_tiles, weight_in))
    w_tri = late_weight[:, : 4 * hidden_width].reshape(width, 2, 2, hidden_width)
    w_tri = w_tri.transpose(0, 2, 3, 1).reshape(width, 4 * hidden_width)
    w_gate = late_weight[:, 4 * hidden_width :]
    sums = weight_sums(grad_tiles, factors, z_norm, grad_w_gate, grad_w_out)
    pieces = sums.reshape(lax.axis_size(ALL), -1, width)
    arrived = lax.all_to_all(pieces, ALL, split_axis=0, concat_axis=0, tiled=True)
    pair_parts = (pair_rep[0], grad_tiles, factors, grad_gate, w_tri, w_gate, gain_in)
    grad_pair = pair_grad(0, z_norm.reshape(pair_rep.shape[1:]), *pair_parts)
    arrived, grad_pair = lax.optimization_barrier((arrived, grad_pair))
    spread = jnp.broadcast_to(jnp.sum(arrived, axis=0, keepdims=True), pieces.shape)
    totals = lax.all_to_all(spread, ALL, split_axis=0, concat_axis=0, tiled=True)
    grad_pair = pair_grad(1, grad_pair, *pair_parts)
    grad_w_in, grad_w_out, grad_g_in, grad_g_out = finish(
        totals.reshape(sums.shape), weight_in, weight_out, gain_in, gain_out
    )
    return (mixed[None], grad_pair[None], grad_w_in, grad_w_out, grad_g_in, grad_g_out)


def solution(mesh):
    return jax.shard_map(
        on_device,
        mesh=mesh,
        in_specs=(
            P("grp", "row", "col", None),
            P("grp", "row", "col", None),
            P(),
            P(),
            P(),
            P(),
            P(),
        ),
        out_specs=(P("grp", "row", "col", None), P("grp", "row", "col", None), P(), P(), P(), P()),
        check_vma=False,
    )
```
